512 devices in a mesh: row: 16 (over x, y_lo), blk: 32 (over y_hi, z, core).
Axes of the slice: x: 4, y: 8 (y_hi: 2, y_lo: 4; y = y_hi * 4 + y_lo), z: 8, core: 2. Of those that a mesh axis runs over, the one named last changes fastest.
Arguments:
- cells: bfloat16 [131072, 768], P(('row', 'blk')), may hold values from -12 to 12
- tile_rows: int32 [6144], P(('row', 'blk')), may hold values from 0 to 1, as said below
- tile_cols: int32 [6144], P(('row', 'blk')), may hold values from 0 to 5, as said below
- tile_count: int32 [512], P(('row', 'blk')), may hold values from 6 to 12, as said below
- halo_blocks: int32 [512], P(('row', 'blk')), may hold values from 0 to 1, as said below
- tile_vals: bfloat16 [6144, 128, 128], P(('row', 'blk')), may hold values from -0.375 to 0.375
- pool_ids: int32 [131072], P(('row', 'blk')), may hold values from 0 to 15, as said below
- w_msg: bfloat16 [768, 768], replicated, may hold values from -0.21875 to 0.21875
- w_query: bfloat16 [768, 768], replicated, may hold values from -1 to 2
- cotangent: bfloat16 [131072, 768], P(('row', 'blk')), may hold values from -6 to 6
Outputs:
- passed: bfloat16 [131072, 768], P(('row', 'blk'))
- attended: bfloat16 [131072, 768], P(('row', 'blk'))
- grad_cells: bfloat16 [131072, 768], P(('row', 'blk'))
The draws below stay inside these ranges and needn't reach their ends.
Inputs may be any that keep to these rules, and one draw needn't show every extreme that they name: `tile_rows`: slot i of a partition's 12 slots, for i < 2, has row i. `tile_cols`: slot i of a partition, for i < 6, has column i; later slots have columns below 2. `tile_count`: slots of a partition at or beyond its count are unused. `halo_blocks`: distinct within one partition. `pool_ids`: every supernode of a partition has at least one of its cells; the first two cells of a partition lie in supernodes 0 and 1.
All inputs are finite; a program needn't handle non-finite values.
Results may differ from the reference program's by a relative error of at most 0.04.
The reference program's roundings to bfloat16 on the way count: a program that leaves them out, or rounds other values in their place, can miss the bound.
Values may be sent and summed in bfloat16 or wider, within the bound.
No kernel may reach another device: no remote copies, remote signals or barrier semaphores. Data moves between devices by JAX's collectives and lax.ppermute only.
A program may use at most 64 MiB of HBM per device.

```python
import math
import jax
import jax.numpy as jnp
from jax import lax

D = 768
HEADS = 12
HEAD = 64
BLOCK = 128
NB = 2
HB = 1
SN_DEV = 16
GRID = 512
EXT = 6
TILES = 12
CELL_DEV = 256
CELLS = 131072
TILE_ALL = 6144
N_ROW = 16
N_BLK = 32


def draw_cells(key, part):
    base = jnp.clip(jax.random.normal(key, (CELLS, D), jnp.float32), -6.0, 6.0)
    return base.astype(jnp.bfloat16)


def draw_tile_rows(key, part):
    slot_index = jnp.arange(TILES, dtype=jnp.int32)[None, :]
    random_rows = jax.random.randint(key, (GRID, TILES), 0, NB, dtype=jnp.int32)
    return jnp.where(slot_index < NB, slot_index, random_rows).reshape(-1)


def draw_tile_cols(key, part):
    slot_index = jnp.arange(TILES, dtype=jnp.int32)[None, :]
    random_cols = jax.random.randint(jax.random.fold_in(key, 11), (GRID, TILES), 0, NB, dtype=jnp.int32)
    return jnp.where(slot_index < NB + 4 * HB, slot_index, random_cols).reshape(-1)


def draw_tile_count(key, part):
    heavy_mask = jax.random.randint(key, (GRID,), 0, 8, dtype=jnp.int32) == 0
    counts = jnp.where(heavy_mask, TILES, NB + 4 * HB).astype(jnp.int32)
    return counts.at[0].set(TILES).at[1].set(NB + 4 * HB)


def draw_halo_blocks(key, part):
    scores_int = jax.random.randint(key, (GRID, NB), 0, 1 << 20, dtype=jnp.int32) * NB + jnp.arange(NB, dtype=jnp.int32)[None, :]
    ordering = jnp.argsort(scores_int, axis=1, stable=True)
    return ordering[:, :HB].astype(jnp.int32).reshape(-1)


def draw_pool_ids(key, part):
    first_key, second_key = jax.random.split(key)
    labels = jax.random.randint(first_key, (GRID, CELL_DEV), 0, SN_DEV, dtype=jnp.int32)
    ranking = jax.random.randint(second_key, (GRID, CELL_DEV - 2), 0, 1 << 16, dtype=jnp.int32) * CELL_DEV + jnp.arange(CELL_DEV - 2, dtype=jnp.int32)[None, :]
    ordering = jnp.argsort(ranking, axis=1, stable=True)[:, :SN_DEV].astype(jnp.int32) + 2
    device_rows = jnp.broadcast_to(jnp.arange(GRID, dtype=jnp.int32)[:, None], (GRID, SN_DEV))
    labels = labels.at[device_rows, ordering].set(jnp.broadcast_to(jnp.arange(SN_DEV, dtype=jnp.int32)[None, :], (GRID, SN_DEV)))
    labels = labels.at[:, 0].set(0).at[:, 1].set(1)
    return labels.reshape(-1)


def draw_w_query(key, part):
    first_key = jax.random.fold_in(key, 0)
    noise = jnp.clip(jax.random.normal(first_key, (D, D), jnp.float32) * (2.0 / math.sqrt(D)), -1.0, 1.0)
    return noise.astype(jnp.bfloat16)


def block_levels(stream_key, extent, cuts, low, largest):
    def one(position, blocks):
        steps = jax.random.uniform(jax.random.fold_in(jax.random.fold_in(stream_key, 6), position), (blocks,), jnp.float32, low / len(cuts), largest / len(cuts))
        return jnp.repeat(jnp.exp(steps), extent[position] // blocks).reshape((-1,) + (1,) * (len(extent) - position - 1))

    loudness = one(*cuts[0])
    for cut in cuts[1:]:
        loudness = loudness * one(*cut)
    return loudness


def centred(rng, dims, deviation, bound, shards=(), held_as=jnp.bfloat16):
    values = deviation * jax.random.normal(rng, dims, jnp.float32)
    if shards:
        values = values * block_levels(rng, dims, shards, -0.22, 0.18)
    return jnp.clip(values, -bound, bound).astype(held_as)


def setup_inputs(seed: int = 0) -> dict:
    seeds = jax.random.split(jax.random.key(seed), 11)
    cells = draw_cells(jax.random.fold_in(seeds[10], 71), 0)
    tile_rows = draw_tile_rows(jax.random.fold_in(seeds[10], 71), 0)
    tile_cols = draw_tile_cols(jax.random.fold_in(seeds[10], 71), 0)
    tile_count = draw_tile_count(jax.random.fold_in(seeds[10], 71), 0)
    halo_blocks = draw_halo_blocks(jax.random.fold_in(seeds[10], 71), 0)
    tile_vals = centred(seeds[5], (TILE_ALL, BLOCK, BLOCK), (2 * BLOCK) ** -0.5, 0.375, ((0, 512),))
    pool_ids = draw_pool_ids(jax.random.fold_in(seeds[10], 71), 0)
    w_msg = centred(seeds[7], (D, D), D ** -0.5, 0.21875)
    w_query = draw_w_query(jax.random.fold_in(seeds[10], 71), 0)
    cotangent = centred(seeds[9], (CELLS, D), 1.0, 6.0, ((0, 512),))
    return dict(cells=cells, tile_rows=tile_rows, tile_cols=tile_cols, tile_count=tile_count, halo_blocks=halo_blocks, tile_vals=tile_vals, pool_ids=pool_ids, w_msg=w_msg, w_query=w_query, cotangent=cotangent)


def silu_slope(values):
    sigma = jax.nn.sigmoid(values)
    return sigma * (1.0 + values * (1.0 - sigma))

def shift_grid(grid, row_step, col_step):
    padded = jnp.pad(grid, ((1, 1), (1, 1)) + ((0, 0),) * (grid.ndim - 2))
    return padded[1 - row_step:1 - row_step + N_ROW, 1 - col_step:1 - col_step + N_BLK]

def pick_rows(source, indices):
    return source[indices]

def reference(cells, tile_rows, tile_cols, tile_count, halo_blocks, tile_vals, pool_ids, w_msg, w_query, cotangent):
    grid_count = N_ROW * N_BLK
    blocks = cells.reshape(grid_count, NB, BLOCK, D)
    halo_index = halo_blocks.reshape(grid_count, HB).astype(jnp.int32)
    boundary = jax.vmap(pick_rows)(blocks, halo_index)
    bound_grid = boundary.reshape(N_ROW, N_BLK, HB, BLOCK, D)
    extended = jnp.concatenate([blocks.reshape(N_ROW, N_BLK, NB, BLOCK, D), shift_grid(bound_grid, 1, 0), shift_grid(bound_grid, -1, 0), shift_grid(bound_grid, 0, 1), shift_grid(bound_grid, 0, -1)], axis=2).reshape(grid_count, EXT, BLOCK, D)
    rows_dev = tile_rows.reshape(grid_count, TILES)
    cols_dev = tile_cols.reshape(grid_count, TILES)
    vals_dev = tile_vals.reshape(grid_count, TILES, BLOCK, BLOCK)
    live_mask = (jnp.arange(TILES, dtype=jnp.int32)[None, :] < tile_count[:, None]).astype(jnp.float32)

    def forward_tiles(inputs):
        ext_dev, row_ids, col_ids, tile_block, alive_mask = inputs
        picked = ext_dev[col_ids].astype(jnp.float32)
        product = jnp.einsum('tab,tbd->tad', tile_block.astype(jnp.float32), picked) * alive_mask[:, None, None]
        choose = (row_ids[None, :] == jnp.arange(NB, dtype=jnp.int32)[:, None]).astype(jnp.float32)
        return jnp.einsum('nt,tad->nad', choose, product)
    message = lax.map(forward_tiles, (extended, rows_dev, cols_dev, vals_dev, live_mask)).astype(jnp.bfloat16).reshape(CELLS, D)
    hidden = jnp.dot(message, w_msg, preferred_element_type=jnp.float32)
    passed = (cells.astype(jnp.float32) + jax.nn.silu(hidden)).astype(jnp.bfloat16)
    member = (pool_ids.reshape(grid_count, 1, CELL_DEV) == jnp.arange(SN_DEV, dtype=jnp.int32)[None, :, None]).astype(jnp.float32)
    counts = lax.optimization_barrier(jnp.sum(member, axis=2))
    pooled = jnp.einsum('dsc,dcf->dsf', member, passed.reshape(grid_count, CELL_DEV, D).astype(jnp.float32))
    supern = (pooled / jnp.sqrt(counts)[:, :, None]).astype(jnp.bfloat16)
    query_proj = jnp.dot(passed, w_query, preferred_element_type=jnp.float32).astype(jnp.bfloat16)
    score_scale = HEAD ** (-0.5)

    def attend(inputs):
        query_row, keys_row, cot_row = inputs
        queries = query_row.reshape(-1, HEADS, HEAD).astype(jnp.float32)
        key_rows = keys_row.reshape(-1, HEADS, HEAD).astype(jnp.float32)
        grads = cot_row.reshape(-1, HEADS, HEAD).astype(jnp.float32)
        scores = jnp.einsum('qhe,khe->hqk', queries, key_rows) * score_scale
        weights = jnp.exp(scores - lax.optimization_barrier(jnp.max(scores, axis=2, keepdims=True)))
        weights = weights / lax.optimization_barrier(jnp.sum(weights, axis=2, keepdims=True))
        rounded = weights.astype(jnp.bfloat16).astype(jnp.float32)
        values_sum = jnp.einsum('hqk,khe->qhe', rounded, key_rows)
        centre = lax.optimization_barrier(jnp.sum(grads * values_sum, axis=2))
        slope = jnp.einsum('qhe,khe->hqk', grads, key_rows)
        dscore = (weights * (slope - centre.T[:, :, None]) * score_scale).astype(jnp.bfloat16).astype(jnp.float32)
        dquery = jnp.einsum('hqk,khe->qhe', dscore, key_rows).astype(jnp.bfloat16)
        dkey = jnp.einsum('hqk,qhe->khe', dscore, queries) + jnp.einsum('hqk,qhe->khe', rounded, grads)
        return (values_sum.astype(jnp.bfloat16).reshape(-1, D), dquery.reshape(-1, D), dkey.reshape(-1, D))
    attended, dquery, dkey = lax.map(attend, (query_proj.reshape(N_ROW, -1, D), supern.reshape(N_ROW, -1, D), cotangent.reshape(N_ROW, -1, D)))
    attended = attended.reshape(CELLS, D)
    dquery = dquery.reshape(CELLS, D)
    key_grad = dkey.reshape(grid_count, SN_DEV, D)
    pool_grad = (key_grad / jnp.sqrt(counts)[:, :, None]).astype(jnp.bfloat16)
    spread = jnp.einsum('dsc,dsf->dcf', member, pool_grad.astype(jnp.float32)).reshape(CELLS, D)
    through = (cotangent.astype(jnp.float32) + jnp.dot(dquery, w_query.T, preferred_element_type=jnp.float32) + spread).astype(jnp.bfloat16)
    dhidden = (through.astype(jnp.float32) * silu_slope(hidden)).astype(jnp.bfloat16)
    dmessage = jnp.dot(dhidden, w_msg.T, preferred_element_type=jnp.float32).astype(jnp.bfloat16).reshape(grid_count, NB, BLOCK, D)

    def backward_tiles(inputs):
        grad_dev, row_ids, col_ids, tile_block, alive_mask = inputs
        picked = grad_dev[row_ids].astype(jnp.float32)
        product = jnp.einsum('tab,tad->tbd', tile_block.astype(jnp.float32), picked) * alive_mask[:, None, None]
        choose = (col_ids[None, :] == jnp.arange(EXT, dtype=jnp.int32)[:, None]).astype(jnp.float32)
        return jnp.einsum('et,tbd->ebd', choose, product)
    ext_grad = lax.map(backward_tiles, (dmessage, rows_dev, cols_dev, vals_dev, live_mask)).reshape(N_ROW, N_BLK, EXT, BLOCK, D)
    own_grad = ext_grad[:, :, :NB].reshape(grid_count, NB, BLOCK, D)
    from_up = ext_grad[:, :, NB:NB + HB]
    from_down = ext_grad[:, :, NB + HB:NB + 2 * HB]
    from_left = ext_grad[:, :, NB + 2 * HB:NB + 3 * HB]
    from_right = ext_grad[:, :, NB + 3 * HB:NB + 4 * HB]
    returned = shift_grid(from_up, -1, 0) + shift_grid(from_down, 1, 0) + shift_grid(from_left, 0, -1) + shift_grid(from_right, 0, 1)
    placing = (halo_index[:, None, :] == jnp.arange(NB, dtype=jnp.int32)[None, :, None]).astype(jnp.float32)
    summed = through.astype(jnp.float32).reshape(grid_count, NB, BLOCK, D) + own_grad + jnp.einsum('dnh,dhbf->dnbf', placing, returned.reshape(grid_count, HB, BLOCK, D), precision=lax.Precision.HIGHEST)
    grad_cells = summed.astype(jnp.bfloat16).reshape(CELLS, D)
    return (passed, attended, grad_cells)
```

```python
import jax
import jax.numpy as jnp
from jax import lax
from jax.experimental import pallas as pl
from jax.experimental.pallas import tpu as pltpu
from jax.sharding import PartitionSpec as P

D = 768
HEADS = 12
HEAD = 64
BLOCK = 128
NB = 2
SN_DEV = 16
EXT = 6
CELL_DEV = 256
CHIPS = 16
KEYS_CORE = CHIPS * SN_DEV
SCALE = HEAD ** (-0.5)
INTERPRET = False

NT = (((1,), (1,)), ((), ()))
TN = (((0,), (0,)), ((), ()))
NN = (((1,), (0,)), ((), ()))


def dot32(a, b, dims=NN):
    return lax.dot_general(a, b, dims, preferred_element_type=jnp.float32)


def vmem(count):
    return [pl.BlockSpec(memory_space=pltpu.VMEM) for _ in range(count)]


def smem(count):
    return [pl.BlockSpec(memory_space=pltpu.SMEM) for _ in range(count)]


def rows_of(block):
    return pl.ds(pl.multiple_of(block * BLOCK, BLOCK), BLOCK)


def member_of(pool_ref):
    ids = jnp.broadcast_to(pool_ref[...], (SN_DEV, CELL_DEV))
    return ids == lax.broadcasted_iota(jnp.int32, (SN_DEV, CELL_DEV), 0)


def roots_of(member):
    return jnp.sqrt(jnp.sum(member.astype(jnp.float32), axis=1, keepdims=True))


def forward_kernel(
    rows_ref,
    cols_ref,
    count_ref,
    cells_ref,
    up_ref,
    down_ref,
    left_ref,
    right_ref,
    vals_ref,
    pool_ref,
    w_msg_ref,
    w_query_ref,
    passed_ref,
    slope_ref,
    query_ref,
    table_ref,
    acc_ref,
):
    acc_ref[0:BLOCK, :] = dot32(vals_ref[0], cells_ref[0:BLOCK, :])
    acc_ref[BLOCK:, :] = dot32(vals_ref[1], cells_ref[BLOCK:, :])

    def add_tile(number, carry):
        picked = cells_ref[rows_of(cols_ref[number]), :]
        acc_ref[rows_of(rows_ref[number]), :] += dot32(vals_ref[number], picked)
        return carry

    lax.fori_loop(EXT, count_ref[0], add_tile, 0)
    for slot, ref in ((2, up_ref), (3, down_ref), (4, left_ref), (5, right_ref)):
        acc_ref[rows_of(rows_ref[slot]), :] += dot32(vals_ref[slot], ref[...])
    hidden = dot32(acc_ref[...].astype(jnp.bfloat16), w_msg_ref[...])
    sigma = 1.0 / (1.0 + jnp.exp(-hidden))
    slope_ref[...] = sigma * (1.0 + hidden * (1.0 - sigma))
    passed = (cells_ref[...].astype(jnp.float32) + hidden * sigma).astype(jnp.bfloat16)
    passed_ref[...] = passed
    member = member_of(pool_ref)
    pooled = dot32(member.astype(jnp.bfloat16), passed)
    supern = (pooled / roots_of(member)).astype(jnp.bfloat16)
    for chip in range(CHIPS):
        table_ref[chip] = supern
    query_ref[...] = (dot32(passed, w_query_ref[...]) * SCALE).astype(jnp.bfloat16)


def attention_kernel(
    query_ref,
    cot_ref,
    own_ref,
    other_ref,
    attended_ref,
    dquery_ref,
    grad_own_ref,
    grad_other_ref,
):
    lanes = lax.broadcasted_iota(jnp.int32, (CELL_DEV, 2 * HEAD), 1)
    for pair in range(HEADS // 2):
        cols = slice(pair * 2 * HEAD, (pair + 1) * 2 * HEAD)
        keys = jnp.concatenate([own_ref[:, cols], other_ref[:, cols]], axis=0)
        keys_t = keys.T
        query, cot = query_ref[:, cols], cot_ref[:, cols]
        values, dquery, key_grad = [], [], None
        for half in range(2):
            inside = (lanes >= half * HEAD) & (lanes < (half + 1) * HEAD)
            q = jnp.where(inside, query, jnp.zeros_like(query))
            g = jnp.where(inside, cot, jnp.zeros_like(cot))
            scores = dot32(keys, q, NT)
            slope = dot32(keys, g, NT)
            probs = jnp.exp(scores - jnp.max(scores, axis=0, keepdims=True))
            probs = probs * (1.0 / jnp.sum(probs, axis=0, keepdims=True))
            rounded = probs.astype(jnp.bfloat16)
            centre = jnp.sum(rounded.astype(jnp.float32) * slope, axis=0, keepdims=True)
            dscore = (probs * (slope - centre)).astype(jnp.bfloat16)
            head_t = keys_t[half * HEAD : (half + 1) * HEAD, :]
            values.append(dot32(head_t, rounded))
            dquery.append(dot32(head_t, dscore))
            part = dot32(dscore, q) + dot32(rounded, g)
            key_grad = part if key_grad is None else key_grad + part
        attended_ref[:, cols] = jnp.concatenate(values, axis=0).T.astype(jnp.bfloat16)
        dquery_ref[:, cols] = (jnp.concatenate(dquery, axis=0) * SCALE).T.astype(jnp.bfloat16)
        grad_own_ref[:, cols] = key_grad[:KEYS_CORE]
        grad_other_ref[:, cols] = key_grad[KEYS_CORE:].astype(jnp.bfloat16)


def query_back_kernel(dquery_ref, w_query_ref, cot_ref, out_ref):
    out_ref[...] = cot_ref[...].astype(jnp.float32) + dot32(dquery_ref[...], w_query_ref[...], NT)


def backward_kernel(
    rows_ref,
    cols_ref,
    count_ref,
    base_ref,
    parts_ref,
    pool_ref,
    slope_ref,
    w_msg_ref,
    vals_ref,
    own_ref,
    up_ref,
    down_ref,
    left_ref,
    right_ref,
    dmsg_ref,
):
    key_grad = jnp.sum(parts_ref[...].astype(jnp.float32), axis=0)
    member = member_of(pool_ref)
    pool_grad = (key_grad / roots_of(member)).astype(jnp.bfloat16)
    spread = dot32(member.astype(jnp.bfloat16), pool_grad, TN)
    through = (base_ref[...] + spread).astype(jnp.bfloat16).astype(jnp.float32)
    dhidden = (through * slope_ref[...]).astype(jnp.bfloat16)
    dmsg_ref[...] = dot32(dhidden, w_msg_ref[...], NT).astype(jnp.bfloat16)
    for slot, ref in ((2, up_ref), (3, down_ref), (4, left_ref), (5, right_ref)):
        picked = dmsg_ref[rows_of(rows_ref[slot]), :]
        ref[...] = dot32(vals_ref[slot], picked, TN).astype(jnp.bfloat16)
    own_ref[0:BLOCK, :] = through[0:BLOCK] + dot32(vals_ref[0], dmsg_ref[0:BLOCK, :], TN)
    own_ref[BLOCK:, :] = through[BLOCK:] + dot32(vals_ref[1], dmsg_ref[BLOCK:, :], TN)

    def back_tile(number, carry):
        picked = dmsg_ref[rows_of(rows_ref[number]), :]
        own_ref[rows_of(cols_ref[number]), :] += dot32(vals_ref[number], picked, TN)
        return carry

    lax.fori_loop(EXT, count_ref[0], back_tile, 0)


def final_kernel(halo_ref, own_ref, a_ref, b_ref, c_ref, d_ref, out_ref):
    returned = (a_ref[...].astype(jnp.float32) + b_ref[...].astype(jnp.float32)) + (
        c_ref[...].astype(jnp.float32) + d_ref[...].astype(jnp.float32)
    )
    out_ref[...] = own_ref[...].astype(jnp.bfloat16)
    rows = rows_of(halo_ref[0])
    out_ref[rows, :] = (own_ref[rows, :] + returned).astype(jnp.bfloat16)


def struct(shape, dtype=jnp.bfloat16):
    return jax.ShapeDtypeStruct(shape, dtype)


def shifted(value, axis, step):
    count = lax.axis_size(axis)
    first, last = max(0, -step), min(count, count - step)
    return lax.ppermute(value, axis, [(i, i + step) for i in range(first, last)])


def swapped(value):
    count = lax.axis_size("blk")
    return lax.ppermute(value, "blk", [(i, i ^ 1) for i in range(count)])


def exchanged(value):
    count = lax.axis_size("blk")
    groups = [list(range(core, count, 2)) for core in range(2)]
    return lax.all_to_all(value, "blk", 0, 0, axis_index_groups=groups)


def body(
    cells,
    tile_rows,
    tile_cols,
    tile_count,
    halo_blocks,
    tile_vals,
    pool_ids,
    w_msg,
    w_query,
    cotangent,
):
    f32 = jnp.float32
    boundary = lax.dynamic_slice_in_dim(cells, halo_blocks[0] * BLOCK, BLOCK, 0)
    halos = [
        shifted(boundary, "row", 1),
        shifted(boundary, "row", -1),
        shifted(boundary, "blk", 1),
        shifted(boundary, "blk", -1),
    ]
    pool = pool_ids.reshape(1, CELL_DEV)
    passed, slope, query, table = pl.pallas_call(
        forward_kernel,
        name="forward",
        in_specs=smem(3) + vmem(9),
        out_specs=vmem(4),
        out_shape=(
            struct((CELL_DEV, D)),
            struct((CELL_DEV, D), f32),
            struct((CELL_DEV, D)),
            struct((CHIPS, SN_DEV, D)),
        ),
        scratch_shapes=[pltpu.VMEM((CELL_DEV, D), f32)],
        interpret=INTERPRET,
    )(tile_rows, tile_cols, tile_count, cells, *halos, tile_vals, pool, w_msg, w_query)
    own_keys = exchanged(table).reshape(KEYS_CORE, D)
    other_keys = swapped(own_keys)
    attended, dquery, grad_own, grad_other = pl.pallas_call(
        attention_kernel,
        name="attention",
        in_specs=vmem(4),
        out_specs=vmem(4),
        out_shape=(
            struct((CELL_DEV, D)),
            struct((CELL_DEV, D)),
            struct((KEYS_CORE, D), f32),
            struct((KEYS_CORE, D)),
        ),
        interpret=INTERPRET,
    )(query, cotangent, own_keys, other_keys)
    received = swapped(grad_other)
    base = pl.pallas_call(
        query_back_kernel,
        name="query_back",
        in_specs=vmem(3),
        out_specs=vmem(1)[0],
        out_shape=struct((CELL_DEV, D), f32),
        cost_estimate=pl.CostEstimate(
            flops=2 * CELL_DEV * D * D, bytes_accessed=3 * 1024 * 1024, transcendentals=0
        ),
        interpret=INTERPRET,
    )(dquery, w_query, cotangent)
    chip_sum = (grad_own + received.astype(f32)).astype(jnp.bfloat16)
    parts = exchanged(chip_sum.reshape(CHIPS, SN_DEV, D))
    own, up, down, left, right = pl.pallas_call(
        backward_kernel,
        name="backward",
        in_specs=smem(3) + vmem(6),
        out_specs=vmem(5),
        out_shape=(struct((CELL_DEV, D), f32),) + (struct((BLOCK, D)),) * 4,
        scratch_shapes=[pltpu.VMEM((CELL_DEV, D), jnp.bfloat16)],
        interpret=INTERPRET,
    )(tile_rows, tile_cols, tile_count, base, parts, pool, slope, w_msg, tile_vals)
    returned = [
        shifted(up, "row", -1),
        shifted(down, "row", 1),
        shifted(left, "blk", -1),
        shifted(right, "blk", 1),
    ]
    grad_cells = pl.pallas_call(
        final_kernel,
        name="final",
        in_specs=smem(1) + vmem(5),
        out_specs=vmem(1)[0],
        out_shape=struct((CELL_DEV, D)),
        interpret=INTERPRET,
    )(halo_blocks, own, *returned)
    return passed, attended, grad_cells


def solution(mesh):
    cells = P(("row", "blk"), None)
    flat = P(("row", "blk"))
    return jax.shard_map(
        body,
        mesh=mesh,
        in_specs=(
            cells,
            flat,
            flat,
            flat,
            flat,
            P(("row", "blk"), None, None),
            flat,
            P(),
            P(),
            cells,
        ),
        out_specs=(cells, cells, cells),
        check_vma=False,
    )
```

```python
import jax
import jax.numpy as jnp
from jax import lax
from jax.experimental import pallas as pl
from jax.experimental.pallas import tpu as pltpu
from jax.sharding import PartitionSpec as P

D = 768
HEADS = 12
HEAD = 64
BLOCK = 128
NB = 2
SN_DEV = 16
EXT = 6
CELL_DEV = 256
CHIPS = 16
KEYS_CORE = CHIPS * SN_DEV
SCALE = HEAD ** (-0.5)
INTERPRET = False
SCORES_MIB = 50

NT = (((1,), (1,)), ((), ()))
TN = (((0,), (0,)), ((), ()))
NN = (((1,), (0,)), ((), ()))


def dot32(a, b, dims=NN):
    return lax.dot_general(a, b, dims, preferred_element_type=jnp.float32)


def vmem(count):
    return [pl.BlockSpec(memory_space=pltpu.VMEM) for _ in range(count)]


def hbm(count):
    return [pl.BlockSpec(memory_space=pltpu.HBM) for _ in range(count)]


def smem(count):
    return [pl.BlockSpec(memory_space=pltpu.SMEM) for _ in range(count)]


def rows_of(block):
    return pl.ds(pl.multiple_of(block * BLOCK, BLOCK), BLOCK)


def member_of(pool_ref):
    ids = jnp.broadcast_to(pool_ref[...], (SN_DEV, CELL_DEV))
    return ids == lax.broadcasted_iota(jnp.int32, (SN_DEV, CELL_DEV), 0)


def roots_of(member):
    return jnp.sqrt(jnp.sum(member.astype(jnp.float32), axis=1, keepdims=True))


def halo_slots():
    odd_row, odd_blk = lax.axis_index("row") % 2, lax.axis_index("blk") % 2
    return (2 + odd_row, 3 - odd_row, 4 + odd_blk, 5 - odd_blk)


def boundary_kernel(halo_ref, cells_ref, out_ref, sem):
    copy = pltpu.make_async_copy(cells_ref.at[rows_of(halo_ref[0])], out_ref, sem)
    copy.start()
    copy.wait()


def own_tiles_kernel(rows_ref, cols_ref, count_ref, cells_ref, vals_ref, acc_ref):
    acc_ref[0:BLOCK, :] = dot32(vals_ref[0], cells_ref[0:BLOCK, :])
    acc_ref[BLOCK:, :] = dot32(vals_ref[1], cells_ref[BLOCK:, :])

    def add_tile(number, carry):
        picked = cells_ref[rows_of(cols_ref[number]), :]
        acc_ref[rows_of(rows_ref[number]), :] += dot32(vals_ref[number], picked)
        return carry

    lax.fori_loop(EXT, count_ref[0], add_tile, 0)


def forward_kernel(
    rows_ref,
    own_ref,
    cells_ref,
    halo0_ref,
    halo1_ref,
    halo2_ref,
    halo3_ref,
    vals_ref,
    pool_ref,
    w_msg_ref,
    passed_ref,
    hidden_ref,
    table_ref,
    acc_ref,
):
    acc_ref[...] = own_ref[...]
    for slot, ref in zip(halo_slots(), (halo0_ref, halo1_ref, halo2_ref, halo3_ref)):
        acc_ref[rows_of(rows_ref[slot]), :] += dot32(vals_ref[slot], ref[...])
    hidden = dot32(acc_ref[...].astype(jnp.bfloat16), w_msg_ref[...])
    hidden_ref[...] = hidden
    silu = hidden / (1.0 + jnp.exp(-hidden))
    passed = (cells_ref[...].astype(jnp.float32) + silu).astype(jnp.bfloat16)
    passed_ref[...] = passed
    member = member_of(pool_ref)
    pooled = dot32(member.astype(jnp.bfloat16), passed)
    supern = (pooled / roots_of(member)).astype(jnp.bfloat16)
    for chip in range(CHIPS):
        table_ref[chip] = supern


def query_kernel(passed_ref, hidden_ref, w_query_ref, query_ref, slope_ref):
    query_ref[...] = (dot32(passed_ref[...], w_query_ref[...]) * SCALE).astype(jnp.bfloat16)
    hidden = hidden_ref[...]
    sigma = 1.0 / (1.0 + jnp.exp(-hidden))
    slope_ref[...] = sigma * (1.0 + hidden * (1.0 - sigma))


def half_lanes(value, half):
    lanes = lax.broadcasted_iota(jnp.int32, value.shape, 1)
    inside = (lanes >= half * HEAD) & (lanes < (half + 1) * HEAD)
    return jnp.where(inside, value, jnp.zeros_like(value))


def pair_cols(pair):
    return slice(pair * 2 * HEAD, (pair + 1) * 2 * HEAD)


def scores_kernel(
    query_ref,
    cot_ref,
    own_ref,
    other_ref,
    weights_ref,
    grad_own_ref,
    grad_other_ref,
    weights_buf,
    sems,
):
    copies = []
    for pair in range(HEADS // 2):
        cols = pair_cols(pair)
        keys = jnp.concatenate([own_ref[:, cols], other_ref[:, cols]], axis=0)
        key_grad = None
        for half in range(2):
            head = 2 * pair + half
            q = half_lanes(query_ref[:, cols], half)
            g = half_lanes(cot_ref[:, cols], half)
            scores = dot32(keys, q, NT)
            slope = dot32(keys, g, NT)
            probs = jnp.exp(scores - jnp.max(scores, axis=0, keepdims=True))
            probs = probs * (1.0 / jnp.sum(probs, axis=0, keepdims=True))
            rounded = probs.astype(jnp.bfloat16)
            centre = jnp.sum(rounded.astype(jnp.float32) * slope, axis=0, keepdims=True)
            dscore = (probs * (slope - centre)).astype(jnp.bfloat16)
            for kind, weights in enumerate((rounded, dscore)):
                weights_buf[kind, head] = weights
                copy = pltpu.make_async_copy(
                    weights_buf.at[kind, head], weights_ref.at[kind, head], sems.at[kind, head]
                )
                copy.start()
                copies.append(copy)
            part = dot32(dscore, q) + dot32(rounded, g)
            key_grad = part if key_grad is None else key_grad + part
        grad_own_ref[:, cols] = key_grad[:KEYS_CORE]
        grad_other_ref[:, cols] = key_grad[KEYS_CORE:].astype(jnp.bfloat16)
    for copy in copies:
        copy.wait()


def chip_sum_kernel(own_ref, received_ref, out_ref):
    for chip in range(CHIPS):
        rows = slice(chip * SN_DEV, (chip + 1) * SN_DEV)
        total = own_ref[rows, :] + received_ref[rows, :].astype(jnp.float32)
        out_ref[chip] = total.astype(jnp.bfloat16)


def values_kernel(
    weights_ref,
    own_ref,
    other_ref,
    cot_ref,
    w_query_ref,
    attended_ref,
    base_ref,
    dquery_ref,
):
    for pair in range(HEADS // 2):
        cols = pair_cols(pair)
        keys_t = jnp.concatenate([own_ref[:, cols], other_ref[:, cols]], axis=0).T
        values, dquery = [], []
        for half in range(2):
            head = 2 * pair + half
            head_t = keys_t[half * HEAD : (half + 1) * HEAD, :]
            values.append(dot32(head_t, weights_ref[0, head]))
            dquery.append(dot32(head_t, weights_ref[1, head]))
        attended_ref[:, cols] = jnp.concatenate(values, axis=0).T.astype(jnp.bfloat16)
        dquery_ref[:, cols] = (jnp.concatenate(dquery, axis=0) * SCALE).T.astype(jnp.bfloat16)
    back = dot32(dquery_ref[...], w_query_ref[...], NT)
    base_ref[...] = cot_ref[...].astype(jnp.float32) + back


def backward_kernel(
    rows_ref,
    base_ref,
    parts_ref,
    pool_ref,
    slope_ref,
    w_msg_ref,
    vals_ref,
    through_ref,
    dmsg_ref,
    back0_ref,
    back1_ref,
    back2_ref,
    back3_ref,
):
    key_grad = jnp.sum(parts_ref[...].astype(jnp.float32), axis=0)
    member = member_of(pool_ref)
    pool_grad = (key_grad / roots_of(member)).astype(jnp.bfloat16)
    spread = dot32(member.astype(jnp.bfloat16), pool_grad, TN)
    through = (base_ref[...] + spread).astype(jnp.bfloat16)
    through_ref[...] = through
    dhidden = (through.astype(jnp.float32) * slope_ref[...]).astype(jnp.bfloat16)
    dmsg_ref[...] = dot32(dhidden, w_msg_ref[...], NT).astype(jnp.bfloat16)
    for slot, ref in zip(halo_slots(), (back0_ref, back1_ref, back2_ref, back3_ref)):
        picked = dmsg_ref[rows_of(rows_ref[slot]), :]
        ref[...] = dot32(vals_ref[slot], picked, TN).astype(jnp.bfloat16)


def own_back_kernel(rows_ref, cols_ref, count_ref, through_ref, dmsg_ref, vals_ref, own_ref):
    through = through_ref[...].astype(jnp.float32)
    own_ref[0:BLOCK, :] = through[0:BLOCK] + dot32(vals_ref[0], dmsg_ref[0:BLOCK, :], TN)
    own_ref[BLOCK:, :] = through[BLOCK:] + dot32(vals_ref[1], dmsg_ref[BLOCK:, :], TN)

    def back_tile(number, carry):
        picked = dmsg_ref[rows_of(rows_ref[number]), :]
        own_ref[rows_of(cols_ref[number]), :] += dot32(vals_ref[number], picked, TN)
        return carry

    lax.fori_loop(EXT, count_ref[0], back_tile, 0)


def final_kernel(halo_ref, own_ref, a_ref, b_ref, c_ref, d_ref, out_ref):
    returned = (a_ref[...].astype(jnp.float32) + b_ref[...].astype(jnp.float32)) + (
        c_ref[...].astype(jnp.float32) + d_ref[...].astype(jnp.float32)
    )
    rows = rows_of(halo_ref[0])
    rest = rows_of(1 - halo_ref[0])
    out_ref[rest, :] = own_ref[rest, :].astype(jnp.bfloat16)
    out_ref[rows, :] = (own_ref[rows, :] + returned).astype(jnp.bfloat16)


def struct(shape, dtype=jnp.bfloat16):
    return jax.ShapeDtypeStruct(shape, dtype)


CELL = struct((CELL_DEV, D))
CELL32 = struct((CELL_DEV, D), jnp.float32)
TILE_FLOPS = 2 * BLOCK * BLOCK * D


def call(kernel, name, scalars, arrays, outs, scratch=(), flops=0, mib=24):
    several = isinstance(outs, tuple)
    specs = vmem(len(outs) if several else 1)
    moved = sum(a.size * a.dtype.itemsize for a in arrays)
    return pl.pallas_call(
        kernel,
        name=name,
        in_specs=smem(len(scalars)) + vmem(len(arrays)),
        out_specs=specs if several else specs[0],
        out_shape=outs,
        scratch_shapes=scratch,
        cost_estimate=pl.CostEstimate(flops=flops, bytes_accessed=moved, transcendentals=0),
        compiler_params=pltpu.CompilerParams(vmem_limit_bytes=mib * 1024 * 1024),
        interpret=INTERPRET,
    )(*scalars, *arrays)


def traded(value, axis, first):
    count = lax.axis_size(axis)
    pairs = [(i, i + 1) for i in range(first, count - 1, 2)]
    return lax.ppermute(value, axis, pairs + [(b, a) for a, b in pairs])


def neighbours(values):
    axes = (("row", 1), ("row", 0), ("blk", 1), ("blk", 0))
    return [traded(value, axis, first) for value, (axis, first) in zip(values, axes)]


def exchanged(value):
    count = lax.axis_size("blk")
    groups = [list(range(core, count, 2)) for core in range(2)]
    return lax.all_to_all(value, "blk", 0, 0, axis_index_groups=groups)


def body(
    cells,
    tile_rows,
    tile_cols,
    tile_count,
    halo_blocks,
    tile_vals,
    pool_ids,
    w_msg,
    w_query,
    cotangent,
):
    f32 = jnp.float32
    boundary = pl.pallas_call(
        boundary_kernel,
        name="boundary",
        in_specs=smem(1) + hbm(1),
        out_specs=vmem(1)[0],
        out_shape=struct((BLOCK, D)),
        scratch_shapes=[pltpu.SemaphoreType.DMA(())],
        compiler_params=pltpu.CompilerParams(vmem_limit_bytes=4 * 1024 * 1024),
        interpret=INTERPRET,
    )(halo_blocks, cells)
    halos = neighbours([boundary] * 4)
    pool = pool_ids.reshape(1, CELL_DEV)
    tiles = (tile_rows, tile_cols, tile_count)
    own_message = call(
        own_tiles_kernel, "own_tiles", tiles, (cells, tile_vals), CELL32, flops=4 * TILE_FLOPS
    )
    passed, hidden, table = call(
        forward_kernel,
        "forward",
        (tile_rows,),
        (own_message, cells, *halos, tile_vals, pool, w_msg),
        (CELL, CELL32, struct((CHIPS, SN_DEV, D))),
        scratch=[pltpu.VMEM((CELL_DEV, D), f32)],
        flops=16 * TILE_FLOPS,
    )
    own_keys = exchanged(table).reshape(KEYS_CORE, D)
    query, slope = call(
        query_kernel,
        "query",
        (),
        (passed, hidden, w_query),
        (CELL, CELL32),
        flops=12 * TILE_FLOPS,
    )
    own_keys, query, slope = lax.optimization_barrier((own_keys, query, slope))
    other_keys = traded(own_keys, "blk", 0)
    weights = struct((2, HEADS, 2 * KEYS_CORE, CELL_DEV))
    weights, grad_own, grad_other = pl.pallas_call(
        scores_kernel,
        name="scores",
        in_specs=vmem(4),
        out_specs=hbm(1) + vmem(2),
        out_shape=(weights, CELL32, CELL),
        scratch_shapes=[
            pltpu.VMEM(weights.shape, jnp.bfloat16),
            pltpu.SemaphoreType.DMA((2, HEADS)),
        ],
        cost_estimate=pl.CostEstimate(
            flops=96 * TILE_FLOPS, bytes_accessed=8 << 20, transcendentals=weights.size
        ),
        compiler_params=pltpu.CompilerParams(vmem_limit_bytes=SCORES_MIB * 1024 * 1024),
        interpret=INTERPRET,
    )(query, cotangent, own_keys, other_keys)
    received = traded(grad_other, "blk", 0)
    chip_sum = call(
        chip_sum_kernel,
        "chip_sum",
        (),
        (grad_own, received),
        struct((CHIPS, SN_DEV, D)),
        flops=TILE_FLOPS,
        mib=8,
    )
    parts = exchanged(chip_sum)
    attended, base = call(
        values_kernel,
        "values",
        (),
        (weights, own_keys, other_keys, cotangent, w_query),
        (CELL, CELL32),
        scratch=[pltpu.VMEM((CELL_DEV, D), jnp.bfloat16)],
        flops=60 * TILE_FLOPS,
        mib=32,
    )
    through, dmessage, *backs = call(
        backward_kernel,
        "backward",
        (tile_rows,),
        (base, parts, pool, slope, w_msg, tile_vals),
        (CELL, CELL) + (struct((BLOCK, D)),) * 4,
        flops=16 * TILE_FLOPS,
    )
    returned = neighbours(backs)
    own = call(
        own_back_kernel,
        "own_back",
        tiles,
        (through, dmessage, tile_vals),
        CELL32,
        flops=4 * TILE_FLOPS,
    )
    grad_cells = call(
        final_kernel, "final", (halo_blocks,), (own, *returned), CELL, flops=TILE_FLOPS
    )
    return passed, attended, grad_cells


def solution(mesh):
    cells = P(("row", "blk"), None)
    flat = P(("row", "blk"))
    return jax.shard_map(
        body,
        mesh=mesh,
        in_specs=(
            cells,
            flat,
            flat,
            flat,
            flat,
            P(("row", "blk"), None, None),
            flat,
            P(),
            P(),
            cells,
        ),
        out_specs=(cells, cells, cells),
        check_vma=False,
    )
```

```python
import jax
import jax.numpy as jnp
from jax import lax
from jax.experimental import pallas as pl
from jax.experimental.pallas import tpu as pltpu
from jax.sharding import PartitionSpec as P

D = 768
HEADS = 12
HEAD = 64
BLOCK = 128
NB = 2
SN_DEV = 16
EXT = 6
CELL_DEV = 256
CHIPS = 16
KEYS_CORE = CHIPS * SN_DEV
SCALE = HEAD ** (-0.5)
INTERPRET = False
BOUNDARY_MIB = 60
OWN_MIB = 60
QUERY_MIB = 24
SCORES_MIB = 50
VALUES_MIB = 60

NT = (((1,), (1,)), ((), ()))
TN = (((0,), (0,)), ((), ()))
NN = (((1,), (0,)), ((), ()))


def dot32(a, b, dims=NN):
    return lax.dot_general(a, b, dims, preferred_element_type=jnp.float32)


def vmem(count):
    return [pl.BlockSpec(memory_space=pltpu.VMEM) for _ in range(count)]


def hbm(count):
    return [pl.BlockSpec(memory_space=pltpu.HBM) for _ in range(count)]


def smem(count):
    return [pl.BlockSpec(memory_space=pltpu.SMEM) for _ in range(count)]


def rows_of(block):
    return pl.ds(pl.multiple_of(block * BLOCK, BLOCK), BLOCK)


def member_of(pool_ref):
    ids = jnp.broadcast_to(pool_ref[...], (SN_DEV, CELL_DEV))
    return ids == lax.broadcasted_iota(jnp.int32, (SN_DEV, CELL_DEV), 0)


def roots_of(member):
    return jnp.sqrt(jnp.sum(member.astype(jnp.float32), axis=1, keepdims=True))


def halo_slots():
    odd_row, odd_blk = lax.axis_index("row") % 2, lax.axis_index("blk") % 2
    return (2 + odd_row, 3 - odd_row, 4 + odd_blk, 5 - odd_blk)


def boundary_kernel(halo_ref, cells_ref, out_ref, sem):
    copy = pltpu.make_async_copy(cells_ref.at[rows_of(halo_ref[0])], out_ref, sem)
    copy.start()
    copy.wait()


def own_tiles_kernel(rows_ref, cols_ref, count_ref, cells_ref, vals_ref, acc_ref):
    acc_ref[0:BLOCK, :] = dot32(vals_ref[0], cells_ref[0:BLOCK, :])
    acc_ref[BLOCK:, :] = dot32(vals_ref[1], cells_ref[BLOCK:, :])

    def add_tile(number, carry):
        picked = cells_ref[rows_of(cols_ref[number]), :]
        acc_ref[rows_of(rows_ref[number]), :] += dot32(vals_ref[number], picked)
        return carry

    lax.fori_loop(EXT, count_ref[0], add_tile, 0)


def forward_kernel(
    rows_ref,
    own_ref,
    cells_ref,
    halo0_ref,
    halo1_ref,
    halo2_ref,
    halo3_ref,
    vals_ref,
    pool_ref,
    w_msg_ref,
    passed_ref,
    slope_ref,
    table_ref,
    acc_ref,
):
    acc_ref[...] = own_ref[...]
    for slot, ref in zip(halo_slots(), (halo0_ref, halo1_ref, halo2_ref, halo3_ref)):
        acc_ref[rows_of(rows_ref[slot]), :] += dot32(vals_ref[slot], ref[...])
    hidden = dot32(acc_ref[...].astype(jnp.bfloat16), w_msg_ref[...])
    sigma = 1.0 / (1.0 + jnp.exp(-hidden))
    slope_ref[...] = (sigma * (1.0 + hidden * (1.0 - sigma))).astype(jnp.bfloat16)
    passed = (cells_ref[...].astype(jnp.float32) + hidden * sigma).astype(jnp.bfloat16)
    passed_ref[...] = passed
    member = member_of(pool_ref)
    pooled = dot32(member.astype(jnp.bfloat16), passed)
    supern = (pooled / roots_of(member)).astype(jnp.bfloat16)
    for chip in range(CHIPS):
        table_ref[chip] = supern


def query_kernel(passed_ref, w_query_ref, query_ref):
    query_ref[...] = (dot32(passed_ref[...], w_query_ref[...]) * SCALE).astype(jnp.bfloat16)


def half_lanes(value, half):
    lanes = lax.broadcasted_iota(jnp.int32, value.shape, 1)
    inside = (lanes >= half * HEAD) & (lanes < (half + 1) * HEAD)
    return jnp.where(inside, value, jnp.zeros_like(value))


def pair_cols(pair):
    return slice(pair * 2 * HEAD, (pair + 1) * 2 * HEAD)


def scores_kernel(
    query_ref,
    cot_ref,
    own_ref,
    other_ref,
    weights_ref,
    grad_own_ref,
    grad_other_ref,
    weights_buf,
    sems,
):
    copies = []
    for pair in range(HEADS // 2):
        cols = pair_cols(pair)
        keys = jnp.concatenate([own_ref[:, cols], other_ref[:, cols]], axis=0)
        key_grad = None
        for half in range(2):
            head = 2 * pair + half
            q = half_lanes(query_ref[:, cols], half)
            g = half_lanes(cot_ref[:, cols], half)
            scores = dot32(keys, q, NT)
            slope = dot32(keys, g, NT)
            probs = jnp.exp(scores - jnp.max(scores, axis=0, keepdims=True))
            probs = probs * (1.0 / jnp.sum(probs, axis=0, keepdims=True))
            rounded = probs.astype(jnp.bfloat16)
            centre = jnp.sum(rounded.astype(jnp.float32) * slope, axis=0, keepdims=True)
            dscore = (probs * (slope - centre)).astype(jnp.bfloat16)
            for kind, weights in enumerate((rounded, dscore)):
                weights_buf[kind, head] = weights
                copy = pltpu.make_async_copy(
                    weights_buf.at[kind, head], weights_ref.at[kind, head], sems.at[kind, head]
                )
                copy.start()
                copies.append(copy)
            part = dot32(dscore, q) + dot32(rounded, g)
            key_grad = part if key_grad is None else key_grad + part
        grad_own_ref[:, cols] = key_grad[:KEYS_CORE]
        grad_other_ref[:, cols] = key_grad[KEYS_CORE:].astype(jnp.bfloat16)
    for copy in copies:
        copy.wait()


def chip_sum_kernel(own_ref, received_ref, out_ref):
    for chip in range(CHIPS):
        rows = slice(chip * SN_DEV, (chip + 1) * SN_DEV)
        total = own_ref[rows, :] + received_ref[rows, :].astype(jnp.float32)
        out_ref[chip] = total.astype(jnp.bfloat16)


def values_kernel(
    weights_ref,
    own_ref,
    other_ref,
    cot_ref,
    w_query_ref,
    attended_ref,
    base_ref,
    dquery_ref,
):
    for pair in range(HEADS // 2):
        cols = pair_cols(pair)
        keys_t = jnp.concatenate([own_ref[:, cols], other_ref[:, cols]], axis=0).T
        values, dquery = [], []
        for half in range(2):
            head = 2 * pair + half
            head_t = keys_t[half * HEAD : (half + 1) * HEAD, :]
            values.append(dot32(head_t, weights_ref[0, head]))
            dquery.append(dot32(head_t, weights_ref[1, head]))
        attended_ref[:, cols] = jnp.concatenate(values, axis=0).T.astype(jnp.bfloat16)
        dquery_ref[:, cols] = (jnp.concatenate(dquery, axis=0) * SCALE).T.astype(jnp.bfloat16)
    back = dot32(dquery_ref[...], w_query_ref[...], NT)
    base_ref[...] = (cot_ref[...].astype(jnp.float32) + back).astype(jnp.bfloat16)


def backward_kernel(
    rows_ref,
    base_ref,
    parts_ref,
    pool_ref,
    slope_ref,
    w_msg_ref,
    vals_ref,
    through_ref,
    dmsg_ref,
    back0_ref,
    back1_ref,
    back2_ref,
    back3_ref,
):
    key_grad = jnp.sum(parts_ref[...].astype(jnp.float32), axis=0)
    member = member_of(pool_ref)
    pool_grad = (key_grad / roots_of(member)).astype(jnp.bfloat16)
    spread = dot32(member.astype(jnp.bfloat16), pool_grad, TN)
    through = (base_ref[...].astype(jnp.float32) + spread).astype(jnp.bfloat16)
    through_ref[...] = through
    slope = slope_ref[...].astype(jnp.float32)
    dhidden = (through.astype(jnp.float32) * slope).astype(jnp.bfloat16)
    dmsg_ref[...] = dot32(dhidden, w_msg_ref[...], NT).astype(jnp.bfloat16)
    for slot, ref in zip(halo_slots(), (back0_ref, back1_ref, back2_ref, back3_ref)):
        picked = dmsg_ref[rows_of(rows_ref[slot]), :]
        ref[...] = dot32(vals_ref[slot], picked, TN).astype(jnp.bfloat16)


def own_back_kernel(rows_ref, cols_ref, count_ref, through_ref, dmsg_ref, vals_ref, own_ref):
    through = through_ref[...].astype(jnp.float32)
    own_ref[0:BLOCK, :] = through[0:BLOCK] + dot32(vals_ref[0], dmsg_ref[0:BLOCK, :], TN)
    own_ref[BLOCK:, :] = through[BLOCK:] + dot32(vals_ref[1], dmsg_ref[BLOCK:, :], TN)

    def back_tile(number, carry):
        picked = dmsg_ref[rows_of(rows_ref[number]), :]
        own_ref[rows_of(cols_ref[number]), :] += dot32(vals_ref[number], picked, TN)
        return carry

    lax.fori_loop(EXT, count_ref[0], back_tile, 0)


def final_kernel(halo_ref, own_ref, a_ref, b_ref, c_ref, d_ref, out_ref):
    returned = (a_ref[...].astype(jnp.float32) + b_ref[...].astype(jnp.float32)) + (
        c_ref[...].astype(jnp.float32) + d_ref[...].astype(jnp.float32)
    )
    rows = rows_of(halo_ref[0])
    rest = rows_of(1 - halo_ref[0])
    out_ref[rest, :] = own_ref[rest, :].astype(jnp.bfloat16)
    out_ref[rows, :] = (own_ref[rows, :] + returned).astype(jnp.bfloat16)


def struct(shape, dtype=jnp.bfloat16):
    return jax.ShapeDtypeStruct(shape, dtype)


CELL = struct((CELL_DEV, D))
CELL32 = struct((CELL_DEV, D), jnp.float32)
TILE_FLOPS = 2 * BLOCK * BLOCK * D


def call(kernel, name, scalars, arrays, outs, scratch=(), flops=0, mib=24):
    several = isinstance(outs, tuple)
    specs = vmem(len(outs) if several else 1)
    moved = sum(a.size * a.dtype.itemsize for a in arrays)
    return pl.pallas_call(
        kernel,
        name=name,
        in_specs=smem(len(scalars)) + vmem(len(arrays)),
        out_specs=specs if several else specs[0],
        out_shape=outs,
        scratch_shapes=scratch,
        cost_estimate=pl.CostEstimate(flops=flops, bytes_accessed=moved, transcendentals=0),
        compiler_params=pltpu.CompilerParams(vmem_limit_bytes=mib * 1024 * 1024),
        interpret=INTERPRET,
    )(*scalars, *arrays)


def traded(value, axis, first):
    count = lax.axis_size(axis)
    pairs = [(i, i + 1) for i in range(first, count - 1, 2)]
    return lax.ppermute(value, axis, pairs + [(b, a) for a, b in pairs])


def neighbours(values):
    axes = (("row", 1), ("row", 0), ("blk", 1), ("blk", 0))
    return [traded(value, axis, first) for value, (axis, first) in zip(values, axes)]


def exchanged(value):
    count = lax.axis_size("blk")
    groups = [list(range(core, count, 2)) for core in range(2)]
    return lax.all_to_all(value, "blk", 0, 0, axis_index_groups=groups)


def body(
    cells,
    tile_rows,
    tile_cols,
    tile_count,
    halo_blocks,
    tile_vals,
    pool_ids,
    w_msg,
    w_query,
    cotangent,
):
    f32 = jnp.float32
    boundary = pl.pallas_call(
        boundary_kernel,
        name="boundary",
        in_specs=smem(1) + hbm(1),
        out_specs=vmem(1)[0],
        out_shape=struct((BLOCK, D)),
        scratch_shapes=[pltpu.SemaphoreType.DMA(())],
        compiler_params=pltpu.CompilerParams(vmem_limit_bytes=BOUNDARY_MIB * 1024 * 1024),
        interpret=INTERPRET,
    )(halo_blocks, cells)
    halos = neighbours([boundary] * 4)
    pool = pool_ids.reshape(1, CELL_DEV)
    tiles = (tile_rows, tile_cols, tile_count)
    own_message = call(
        own_tiles_kernel,
        "own_tiles",
        tiles,
        (cells, tile_vals),
        CELL32,
        flops=4 * TILE_FLOPS,
        mib=OWN_MIB,
    )
    passed, slope, table = call(
        forward_kernel,
        "forward",
        (tile_rows,),
        (own_message, cells, *halos, tile_vals, pool, w_msg),
        (CELL, CELL, struct((CHIPS, SN_DEV, D))),
        scratch=[pltpu.VMEM((CELL_DEV, D), f32)],
        flops=16 * TILE_FLOPS,
    )
    own_keys = exchanged(table).reshape(KEYS_CORE, D)
    query = call(
        query_kernel, "query", (), (passed, w_query), CELL, flops=12 * TILE_FLOPS, mib=QUERY_MIB
    )
    own_keys, query = lax.optimization_barrier((own_keys, query))
    other_keys = traded(own_keys, "blk", 0)
    weights = struct((2, HEADS, 2 * KEYS_CORE, CELL_DEV))
    weights, grad_own, grad_other = pl.pallas_call(
        scores_kernel,
        name="scores",
        in_specs=vmem(4),
        out_specs=hbm(1) + vmem(2),
        out_shape=(weights, CELL32, CELL),
        scratch_shapes=[
            pltpu.VMEM(weights.shape, jnp.bfloat16),
            pltpu.SemaphoreType.DMA((2, HEADS)),
        ],
        cost_estimate=pl.CostEstimate(
            flops=96 * TILE_FLOPS, bytes_accessed=8 << 20, transcendentals=weights.size
        ),
        compiler_params=pltpu.CompilerParams(vmem_limit_bytes=SCORES_MIB * 1024 * 1024),
        interpret=INTERPRET,
    )(query, cotangent, own_keys, other_keys)
    received = traded(grad_other, "blk", 0)
    chip_sum = call(
        chip_sum_kernel,
        "chip_sum",
        (),
        (grad_own, received),
        struct((CHIPS, SN_DEV, D)),
        flops=TILE_FLOPS,
        mib=8,
    )
    parts = exchanged(chip_sum)
    attended, base = call(
        values_kernel,
        "values",
        (),
        (weights, own_keys, other_keys, cotangent, w_query),
        (CELL, CELL),
        scratch=[pltpu.VMEM((CELL_DEV, D), jnp.bfloat16)],
        flops=60 * TILE_FLOPS,
        mib=VALUES_MIB,
    )
    through, dmessage, *backs = call(
        backward_kernel,
        "backward",
        (tile_rows,),
        (base, parts, pool, slope, w_msg, tile_vals),
        (CELL, CELL) + (struct((BLOCK, D)),) * 4,
        flops=16 * TILE_FLOPS,
    )
    returned = neighbours(backs)
    own = call(
        own_back_kernel,
        "own_back",
        tiles,
        (through, dmessage, tile_vals),
        CELL32,
        flops=4 * TILE_FLOPS,
    )
    grad_cells = call(
        final_kernel, "final", (halo_blocks,), (own, *returned), CELL, flops=TILE_FLOPS
    )
    return passed, attended, grad_cells


def solution(mesh):
    cells = P(("row", "blk"), None)
    flat = P(("row", "blk"))
    return jax.shard_map(
        body,
        mesh=mesh,
        in_specs=(
            cells,
            flat,
            flat,
            flat,
            flat,
            P(("row", "blk"), None, None),
            flat,
            P(),
            P(),
            cells,
        ),
        out_specs=(cells, cells, cells),
        check_vma=False,
    )
```

```python
import jax
import jax.numpy as jnp
from jax import lax
from jax.experimental import pallas as pl
from jax.experimental.pallas import tpu as pltpu
from jax.sharding import PartitionSpec as P

D = 768
HEADS = 12
HEAD = 64
BLOCK = 128
NB = 2
SN_DEV = 16
EXT = 6
CELL_DEV = 256
CHIPS = 16
KEYS_CORE = CHIPS * SN_DEV
SCALE = HEAD ** (-0.5)
INTERPRET = False
OWN_MIB = 60
FORWARD_MIB = 53
QUERY_MIB = 48
SCORES_MIB = 50
SUM_MIB = 8
VALUES_MIB = 53
BACK_MIB = 24
OWN_BACK_MIB = 24
FINAL_MIB = 24

NT = (((1,), (1,)), ((), ()))
TN = (((0,), (0,)), ((), ()))
NN = (((1,), (0,)), ((), ()))


def dot32(a, b, dims=NN):
    return lax.dot_general(a, b, dims, preferred_element_type=jnp.float32)


def vmem(count):
    return [pl.BlockSpec(memory_space=pltpu.VMEM) for _ in range(count)]


def hbm(count):
    return [pl.BlockSpec(memory_space=pltpu.HBM) for _ in range(count)]


def smem(count):
    return [pl.BlockSpec(memory_space=pltpu.SMEM) for _ in range(count)]


def rows_of(block):
    return pl.ds(pl.multiple_of(block * BLOCK, BLOCK), BLOCK)


def member_of(pool_ref):
    ids = jnp.broadcast_to(pool_ref[...], (SN_DEV, CELL_DEV))
    return ids == lax.broadcasted_iota(jnp.int32, (SN_DEV, CELL_DEV), 0)


def roots_of(member):
    return jnp.sqrt(jnp.sum(member.astype(jnp.float32), axis=1, keepdims=True))


def halo_slots():
    odd_row, odd_blk = lax.axis_index("row") % 2, lax.axis_index("blk") % 2
    return (2 + odd_row, 3 - odd_row, 4 + odd_blk, 5 - odd_blk)


def own_tiles_kernel(rows_ref, cols_ref, count_ref, cells_ref, vals_ref, acc_ref):
    acc_ref[0:BLOCK, :] = dot32(vals_ref[0], cells_ref[0:BLOCK, :])
    acc_ref[BLOCK:, :] = dot32(vals_ref[1], cells_ref[BLOCK:, :])

    def add_tile(number, carry):
        picked = cells_ref[rows_of(cols_ref[number]), :]
        acc_ref[rows_of(rows_ref[number]), :] += dot32(vals_ref[number], picked)
        return carry

    lax.fori_loop(EXT, count_ref[0], add_tile, 0)


def forward_kernel(
    rows_ref,
    own_ref,
    cells_ref,
    halo0_ref,
    halo1_ref,
    halo2_ref,
    halo3_ref,
    vals_ref,
    pool_ref,
    w_msg_ref,
    passed_ref,
    slope_ref,
    table_ref,
    acc_ref,
):
    acc_ref[...] = own_ref[...]
    for slot, ref in zip(halo_slots(), (halo0_ref, halo1_ref, halo2_ref, halo3_ref)):
        acc_ref[rows_of(rows_ref[slot]), :] += dot32(vals_ref[slot], ref[...])
    hidden = dot32(acc_ref[...].astype(jnp.bfloat16), w_msg_ref[...])
    sigma = 1.0 / (1.0 + jnp.exp(-hidden))
    slope_ref[...] = (sigma * (1.0 + hidden * (1.0 - sigma))).astype(jnp.bfloat16)
    passed = (cells_ref[...].astype(jnp.float32) + hidden * sigma).astype(jnp.bfloat16)
    passed_ref[...] = passed
    member = member_of(pool_ref)
    pooled = dot32(member.astype(jnp.bfloat16), passed)
    supern = (pooled / roots_of(member)).astype(jnp.bfloat16)
    for chip in range(CHIPS):
        table_ref[chip] = supern


def query_kernel(passed_ref, w_query_ref, query_ref):
    query_ref[...] = (dot32(passed_ref[...], w_query_ref[...]) * SCALE).astype(jnp.bfloat16)


def half_lanes(value, half):
    lanes = lax.broadcasted_iota(jnp.int32, value.shape, 1)
    inside = (lanes >= half * HEAD) & (lanes < (half + 1) * HEAD)
    return jnp.where(inside, value, jnp.zeros_like(value))


def pair_cols(pair):
    return slice(pair * 2 * HEAD, (pair + 1) * 2 * HEAD)


def scores_kernel(
    query_ref,
    cot_ref,
    keys_ref,
    weights_ref,
    grad_own_ref,
    grad_other_ref,
    weights_buf,
    sems,
):
    first = lax.axis_index("blk") % 2 == 0
    copies = []
    for pair in range(HEADS // 2):
        cols = pair_cols(pair)
        keys = keys_ref[:, cols]
        key_grad = None
        for half in range(2):
            head = 2 * pair + half
            q = half_lanes(query_ref[:, cols], half)
            g = half_lanes(cot_ref[:, cols], half)
            scores = dot32(keys, q, NT)
            slope = dot32(keys, g, NT)
            probs = jnp.exp(scores - jnp.max(scores, axis=0, keepdims=True))
            probs = probs * (1.0 / jnp.sum(probs, axis=0, keepdims=True))
            rounded = probs.astype(jnp.bfloat16)
            centre = jnp.sum(rounded.astype(jnp.float32) * slope, axis=0, keepdims=True)
            dscore = (probs * (slope - centre)).astype(jnp.bfloat16)
            for kind, weights in enumerate((rounded, dscore)):
                weights_buf[kind, head] = weights
                copy = pltpu.make_async_copy(
                    weights_buf.at[kind, head], weights_ref.at[kind, head], sems.at[kind, head]
                )
                copy.start()
                copies.append(copy)
            part = dot32(dscore, q) + dot32(rounded, g)
            key_grad = part if key_grad is None else key_grad + part
        low, high = key_grad[:KEYS_CORE], key_grad[KEYS_CORE:]
        grad_own_ref[:, cols] = jnp.where(first, low, high)
        grad_other_ref[:, cols] = jnp.where(first, high, low).astype(jnp.bfloat16)
    for copy in copies:
        copy.wait()


def chip_sum_kernel(own_ref, both_ref, out_ref):
    partner = (1 - lax.axis_index("blk") % 2) * KEYS_CORE
    for chip in range(CHIPS):
        start = chip * SN_DEV
        received = both_ref[pl.ds(pl.multiple_of(partner + start, SN_DEV), SN_DEV), :]
        total = own_ref[start : start + SN_DEV, :] + received.astype(jnp.float32)
        out_ref[chip] = total.astype(jnp.bfloat16)


def values_kernel(
    weights_ref,
    keys_ref,
    cot_ref,
    w_query_ref,
    attended_ref,
    base_ref,
    dquery_ref,
):
    for pair in range(HEADS // 2):
        cols = pair_cols(pair)
        keys_t = keys_ref[:, cols].T
        values, dquery = [], []
        for half in range(2):
            head = 2 * pair + half
            head_t = keys_t[half * HEAD : (half + 1) * HEAD, :]
            values.append(dot32(head_t, weights_ref[0, head]))
            dquery.append(dot32(head_t, weights_ref[1, head]))
        attended_ref[:, cols] = jnp.concatenate(values, axis=0).T.astype(jnp.bfloat16)
        dquery_ref[:, cols] = (jnp.concatenate(dquery, axis=0) * SCALE).T.astype(jnp.bfloat16)
    back = dot32(dquery_ref[...], w_query_ref[...], NT)
    base_ref[...] = (cot_ref[...].astype(jnp.float32) + back).astype(jnp.bfloat16)


def backward_kernel(
    rows_ref,
    base_ref,
    parts_ref,
    pool_ref,
    slope_ref,
    w_msg_ref,
    vals_ref,
    through_ref,
    dmsg_ref,
    back0_ref,
    back1_ref,
    back2_ref,
    back3_ref,
):
    key_grad = jnp.sum(parts_ref[...].astype(jnp.float32), axis=0)
    member = member_of(pool_ref)
    pool_grad = (key_grad / roots_of(member)).astype(jnp.bfloat16)
    spread = dot32(member.astype(jnp.bfloat16), pool_grad, TN)
    through = (base_ref[...].astype(jnp.float32) + spread).astype(jnp.bfloat16)
    through_ref[...] = through
    slope = slope_ref[...].astype(jnp.float32)
    dhidden = (through.astype(jnp.float32) * slope).astype(jnp.bfloat16)
    dmsg_ref[...] = dot32(dhidden, w_msg_ref[...], NT).astype(jnp.bfloat16)
    for slot, ref in zip(halo_slots(), (back0_ref, back1_ref, back2_ref, back3_ref)):
        picked = dmsg_ref[rows_of(rows_ref[slot]), :]
        ref[...] = dot32(vals_ref[slot], picked, TN).astype(jnp.bfloat16)


def own_back_kernel(rows_ref, cols_ref, count_ref, through_ref, dmsg_ref, vals_ref, own_ref):
    through = through_ref[...].astype(jnp.float32)
    own_ref[0:BLOCK, :] = through[0:BLOCK] + dot32(vals_ref[0], dmsg_ref[0:BLOCK, :], TN)
    own_ref[BLOCK:, :] = through[BLOCK:] + dot32(vals_ref[1], dmsg_ref[BLOCK:, :], TN)

    def back_tile(number, carry):
        picked = dmsg_ref[rows_of(rows_ref[number]), :]
        own_ref[rows_of(cols_ref[number]), :] += dot32(vals_ref[number], picked, TN)
        return carry

    lax.fori_loop(EXT, count_ref[0], back_tile, 0)


def final_kernel(halo_ref, own_ref, a_ref, b_ref, c_ref, d_ref, out_ref):
    returned = (a_ref[...].astype(jnp.float32) + b_ref[...].astype(jnp.float32)) + (
        c_ref[...].astype(jnp.float32) + d_ref[...].astype(jnp.float32)
    )
    rows = rows_of(halo_ref[0])
    rest = rows_of(1 - halo_ref[0])
    out_ref[rest, :] = own_ref[rest, :].astype(jnp.bfloat16)
    out_ref[rows, :] = (own_ref[rows, :] + returned).astype(jnp.bfloat16)


def struct(shape, dtype=jnp.bfloat16):
    return jax.ShapeDtypeStruct(shape, dtype)


CELL = struct((CELL_DEV, D))
CELL32 = struct((CELL_DEV, D), jnp.float32)
TILE_FLOPS = 2 * BLOCK * BLOCK * D


def call(kernel, name, scalars, arrays, outs, scratch=(), flops=0, mib=60):
    several = isinstance(outs, tuple)
    specs = vmem(len(outs) if several else 1)
    moved = sum(a.size * a.dtype.itemsize for a in arrays)
    return pl.pallas_call(
        kernel,
        name=name,
        in_specs=smem(len(scalars)) + vmem(len(arrays)),
        out_specs=specs if several else specs[0],
        out_shape=outs,
        scratch_shapes=scratch,
        cost_estimate=pl.CostEstimate(flops=flops, bytes_accessed=moved, transcendentals=0),
        compiler_params=pltpu.CompilerParams(vmem_limit_bytes=mib * 1024 * 1024),
        interpret=INTERPRET,
    )(*scalars, *arrays)


def traded(value, axis, first):
    count = lax.axis_size(axis)
    pairs = [(i, i + 1) for i in range(first, count - 1, 2)]
    return lax.ppermute(value, axis, pairs + [(b, a) for a, b in pairs])


def neighbours(values):
    axes = (("row", 1), ("row", 0), ("blk", 1), ("blk", 0))
    return [traded(value, axis, first) for value, (axis, first) in zip(values, axes)]


def both_cores(value):
    count = lax.axis_size("blk")
    groups = [[i, i + 1] for i in range(0, count, 2)]
    return lax.all_gather(value, "blk", axis=0, tiled=True, axis_index_groups=groups)


def exchanged(value):
    count = lax.axis_size("blk")
    groups = [list(range(core, count, 2)) for core in range(2)]
    return lax.all_to_all(value, "blk", 0, 0, axis_index_groups=groups)


def body(
    cells,
    tile_rows,
    tile_cols,
    tile_count,
    halo_blocks,
    tile_vals,
    pool_ids,
    w_msg,
    w_query,
    cotangent,
):
    f32 = jnp.float32
    boundary = lax.dynamic_slice_in_dim(cells, halo_blocks[0] * BLOCK, BLOCK, 0)
    halos = neighbours([boundary] * 4)
    pool = pool_ids.reshape(1, CELL_DEV)
    tiles = (tile_rows, tile_cols, tile_count)
    own_message = call(
        own_tiles_kernel,
        "own_tiles",
        tiles,
        (cells, tile_vals),
        CELL32,
        flops=4 * TILE_FLOPS,
        mib=OWN_MIB,
    )
    passed, slope, table = call(
        forward_kernel,
        "forward",
        (tile_rows,),
        (own_message, cells, *halos, tile_vals, pool, w_msg),
        (CELL, CELL, struct((CHIPS, SN_DEV, D))),
        scratch=[pltpu.VMEM((CELL_DEV, D), f32)],
        flops=16 * TILE_FLOPS,
        mib=FORWARD_MIB,
    )
    own_keys = exchanged(table).reshape(KEYS_CORE, D)
    query = call(
        query_kernel, "query", (), (passed, w_query), CELL, flops=12 * TILE_FLOPS, mib=QUERY_MIB
    )
    own_keys, query = lax.optimization_barrier((own_keys, query))
    keys = both_cores(own_keys)
    weights = struct((2, HEADS, 2 * KEYS_CORE, CELL_DEV))
    weights, grad_own, grad_other = pl.pallas_call(
        scores_kernel,
        name="scores",
        in_specs=vmem(3),
        out_specs=hbm(1) + vmem(2),
        out_shape=(weights, CELL32, CELL),
        scratch_shapes=[
            pltpu.VMEM(weights.shape, jnp.bfloat16),
            pltpu.SemaphoreType.DMA((2, HEADS)),
        ],
        cost_estimate=pl.CostEstimate(
            flops=96 * TILE_FLOPS, bytes_accessed=8 << 20, transcendentals=weights.size
        ),
        compiler_params=pltpu.CompilerParams(vmem_limit_bytes=SCORES_MIB * 1024 * 1024),
        interpret=INTERPRET,
    )(query, cotangent, keys)
    both = both_cores(grad_other)
    chip_sum = call(
        chip_sum_kernel,
        "chip_sum",
        (),
        (grad_own, both),
        struct((CHIPS, SN_DEV, D)),
        flops=TILE_FLOPS,
        mib=SUM_MIB,
    )
    parts = exchanged(chip_sum)
    attended, base = call(
        values_kernel,
        "values",
        (),
        (weights, keys, cotangent, w_query),
        (CELL, CELL),
        scratch=[pltpu.VMEM((CELL_DEV, D), jnp.bfloat16)],
        flops=60 * TILE_FLOPS,
        mib=VALUES_MIB,
    )
    through, dmessage, *backs = call(
        backward_kernel,
        "backward",
        (tile_rows,),
        (base, parts, pool, slope, w_msg, tile_vals),
        (CELL, CELL) + (struct((BLOCK, D)),) * 4,
        flops=16 * TILE_FLOPS,
        mib=BACK_MIB,
    )
    returned = neighbours(backs)
    own = call(
        own_back_kernel,
        "own_back",
        tiles,
        (through, dmessage, tile_vals),
        CELL32,
        flops=4 * TILE_FLOPS,
        mib=OWN_BACK_MIB,
    )
    grad_cells = call(
        final_kernel,
        "final",
        (halo_blocks,),
        (own, *returned),
        CELL,
        flops=TILE_FLOPS,
        mib=FINAL_MIB,
    )
    return passed, attended, grad_cells


def solution(mesh):
    cells = P(("row", "blk"), None)
    flat = P(("row", "blk"))
    return jax.shard_map(
        body,
        mesh=mesh,
        in_specs=(
            cells,
            flat,
            flat,
            flat,
            flat,
            P(("row", "blk"), None, None),
            flat,
            P(),
            P(),
            cells,
        ),
        out_specs=(cells, cells, cells),
        check_vma=False,
    )
```

```python
import jax
import jax.numpy as jnp
from jax import lax
from jax.experimental import pallas as pl
from jax.experimental.pallas import tpu as pltpu
from jax.sharding import PartitionSpec as P

D = 768
HEADS = 12
HEAD = 64
BLOCK = 128
SN_DEV = 16
EXT = 6
CELL_DEV = 256
CHIPS = 16
KEYS_CORE = CHIPS * SN_DEV
SCALE = HEAD ** (-0.5)
INTERPRET = False
FORWARD_MIB = 60
QUERY_MIB = 48
SCORES_MIB = 50
SUM_MIB = 8
VALUES_MIB = 53
BACK_MIB = 24
OWN_BACK_MIB = 24
FINAL_MIB = 24

NT = (((1,), (1,)), ((), ()))
TN = (((0,), (0,)), ((), ()))
NN = (((1,), (0,)), ((), ()))


def dot32(a, b, dims=NN):
    return lax.dot_general(a, b, dims, preferred_element_type=jnp.float32)


def vmem(count):
    return [pl.BlockSpec(memory_space=pltpu.VMEM) for _ in range(count)]


def hbm(count):
    return [pl.BlockSpec(memory_space=pltpu.HBM) for _ in range(count)]


def anywhere(count):
    return [pl.BlockSpec(memory_space=pl.ANY) for _ in range(count)]


def smem(count):
    return [pl.BlockSpec(memory_space=pltpu.SMEM) for _ in range(count)]


def rows_of(block):
    return pl.ds(pl.multiple_of(block * BLOCK, BLOCK), BLOCK)


def member_of(pool_ref):
    ids = jnp.broadcast_to(pool_ref[...], (SN_DEV, CELL_DEV))
    return ids == lax.broadcasted_iota(jnp.int32, (SN_DEV, CELL_DEV), 0)


def roots_of(member):
    return jnp.sqrt(jnp.sum(member.astype(jnp.float32), axis=1, keepdims=True))


def halo_slots():
    odd_row, odd_blk = lax.axis_index("row") % 2, lax.axis_index("blk") % 2
    return (2 + odd_row, 3 - odd_row, 4 + odd_blk, 5 - odd_blk)


def forward_kernel(
    rows_ref,
    cols_ref,
    count_ref,
    halo0_ref,
    halo1_ref,
    halo2_ref,
    halo3_ref,
    pool_ref,
    cells_hbm,
    vals_hbm,
    w_msg_hbm,
    passed_hbm,
    slope_hbm,
    table_ref,
    acc_ref,
    cells_ref,
    vals_ref,
    w_msg_ref,
    passed_ref,
    slope_ref,
    sems,
):
    moves = (
        (cells_hbm, cells_ref),
        (vals_hbm, vals_ref),
        (w_msg_hbm, w_msg_ref),
        (passed_ref, passed_hbm),
        (slope_ref, slope_hbm),
    )
    copies = [pltpu.make_async_copy(*move, sems.at[i]) for i, move in enumerate(moves)]
    for copy in copies[:3]:
        copy.start()
    copies[0].wait()
    copies[1].wait()
    acc_ref[0:BLOCK, :] = dot32(vals_ref[0], cells_ref[0:BLOCK, :])
    acc_ref[BLOCK:, :] = dot32(vals_ref[1], cells_ref[BLOCK:, :])

    def add_tile(number, carry):
        picked = cells_ref[rows_of(cols_ref[number]), :]
        acc_ref[rows_of(rows_ref[number]), :] += dot32(vals_ref[number], picked)
        return carry

    lax.fori_loop(EXT, count_ref[0], add_tile, 0)
    for slot, ref in zip(halo_slots(), (halo0_ref, halo1_ref, halo2_ref, halo3_ref)):
        acc_ref[rows_of(rows_ref[slot]), :] += dot32(vals_ref[slot], ref[...])
    copies[2].wait()
    hidden = dot32(acc_ref[...].astype(jnp.bfloat16), w_msg_ref[...])
    sigma = 1.0 / (1.0 + jnp.exp(-hidden))
    slope_ref[...] = (sigma * (1.0 + hidden * (1.0 - sigma))).astype(jnp.bfloat16)
    passed = (cells_ref[...].astype(jnp.float32) + hidden * sigma).astype(jnp.bfloat16)
    passed_ref[...] = passed
    for copy in copies[3:]:
        copy.start()
    member = member_of(pool_ref)
    pooled = dot32(member.astype(jnp.bfloat16), passed)
    supern = (pooled / roots_of(member)).astype(jnp.bfloat16)
    for chip in range(CHIPS):
        table_ref[chip] = supern
    for copy in copies[3:]:
        copy.wait()


def query_kernel(passed_ref, w_query_ref, query_ref):
    query_ref[...] = (dot32(passed_ref[...], w_query_ref[...]) * SCALE).astype(jnp.bfloat16)


def half_lanes(value, half):
    lanes = lax.broadcasted_iota(jnp.int32, value.shape, 1)
    inside = (lanes >= half * HEAD) & (lanes < (half + 1) * HEAD)
    return jnp.where(inside, value, jnp.zeros_like(value))


def pair_cols(pair):
    return slice(pair * 2 * HEAD, (pair + 1) * 2 * HEAD)


def scores_kernel(
    query_ref,
    cot_ref,
    keys_ref,
    weights_ref,
    grad_own_ref,
    grad_other_ref,
    weights_buf,
    sems,
):
    first = lax.axis_index("blk") % 2 == 0
    copies = []
    for pair in range(HEADS // 2):
        cols = pair_cols(pair)
        keys = keys_ref[:, cols]
        key_grad = None
        for half in range(2):
            head = 2 * pair + half
            q = half_lanes(query_ref[:, cols], half)
            g = half_lanes(cot_ref[:, cols], half)
            scores = dot32(keys, q, NT)
            slope = dot32(keys, g, NT)
            probs = jnp.exp(scores - jnp.max(scores, axis=0, keepdims=True))
            probs = probs * (1.0 / jnp.sum(probs, axis=0, keepdims=True))
            rounded = probs.astype(jnp.bfloat16)
            centre = jnp.sum(rounded.astype(jnp.float32) * slope, axis=0, keepdims=True)
            dscore = (probs * (slope - centre)).astype(jnp.bfloat16)
            for kind, weights in enumerate((rounded, dscore)):
                weights_buf[kind, head] = weights
                copy = pltpu.make_async_copy(
                    weights_buf.at[kind, head], weights_ref.at[kind, head], sems.at[kind, head]
                )
                copy.start()
                copies.append(copy)
            part = dot32(dscore, q) + dot32(rounded, g)
            key_grad = part if key_grad is None else key_grad + part
        low, high = key_grad[:KEYS_CORE], key_grad[KEYS_CORE:]
        grad_own_ref[:, cols] = jnp.where(first, low, high)
        grad_other_ref[:, cols] = jnp.where(first, high, low).astype(jnp.bfloat16)
    for copy in copies:
        copy.wait()


def chip_sum_kernel(own_ref, both_ref, out_ref):
    partner = (1 - lax.axis_index("blk") % 2) * KEYS_CORE
    for chip in range(CHIPS):
        start = chip * SN_DEV
        received = both_ref[pl.ds(pl.multiple_of(partner + start, SN_DEV), SN_DEV), :]
        total = own_ref[start : start + SN_DEV, :] + received.astype(jnp.float32)
        out_ref[chip] = total.astype(jnp.bfloat16)


def values_kernel(
    weights_ref,
    keys_ref,
    cot_ref,
    w_query_ref,
    attended_ref,
    base_ref,
    dquery_ref,
):
    for pair in range(HEADS // 2):
        cols = pair_cols(pair)
        keys_t = keys_ref[:, cols].T
        values, dquery = [], []
        for half in range(2):
            head = 2 * pair + half
            head_t = keys_t[half * HEAD : (half + 1) * HEAD, :]
            values.append(dot32(head_t, weights_ref[0, head]))
            dquery.append(dot32(head_t, weights_ref[1, head]))
        attended_ref[:, cols] = jnp.concatenate(values, axis=0).T.astype(jnp.bfloat16)
        dquery_ref[:, cols] = (jnp.concatenate(dquery, axis=0) * SCALE).T.astype(jnp.bfloat16)
    back = dot32(dquery_ref[...], w_query_ref[...], NT)
    base_ref[...] = (cot_ref[...].astype(jnp.float32) + back).astype(jnp.bfloat16)


def backward_kernel(
    rows_ref,
    base_ref,
    parts_ref,
    pool_ref,
    slope_ref,
    w_msg_ref,
    vals_ref,
    through_ref,
    dmsg_ref,
    back0_ref,
    back1_ref,
    back2_ref,
    back3_ref,
):
    key_grad = jnp.sum(parts_ref[...].astype(jnp.float32), axis=0)
    member = member_of(pool_ref)
    pool_grad = (key_grad / roots_of(member)).astype(jnp.bfloat16)
    spread = dot32(member.astype(jnp.bfloat16), pool_grad, TN)
    through = (base_ref[...].astype(jnp.float32) + spread).astype(jnp.bfloat16)
    through_ref[...] = through
    slope = slope_ref[...].astype(jnp.float32)
    dhidden = (through.astype(jnp.float32) * slope).astype(jnp.bfloat16)
    dmsg_ref[...] = dot32(dhidden, w_msg_ref[...], NT).astype(jnp.bfloat16)
    for slot, ref in zip(halo_slots(), (back0_ref, back1_ref, back2_ref, back3_ref)):
        picked = dmsg_ref[rows_of(rows_ref[slot]), :]
        ref[...] = dot32(vals_ref[slot], picked, TN).astype(jnp.bfloat16)


def own_back_kernel(rows_ref, cols_ref, count_ref, through_ref, dmsg_ref, vals_ref, own_ref):
    through = through_ref[...].astype(jnp.float32)
    own_ref[0:BLOCK, :] = through[0:BLOCK] + dot32(vals_ref[0], dmsg_ref[0:BLOCK, :], TN)
    own_ref[BLOCK:, :] = through[BLOCK:] + dot32(vals_ref[1], dmsg_ref[BLOCK:, :], TN)

    def back_tile(number, carry):
        picked = dmsg_ref[rows_of(rows_ref[number]), :]
        own_ref[rows_of(cols_ref[number]), :] += dot32(vals_ref[number], picked, TN)
        return carry

    lax.fori_loop(EXT, count_ref[0], back_tile, 0)


def final_kernel(halo_ref, own_ref, a_ref, b_ref, c_ref, d_ref, out_ref):
    returned = (a_ref[...].astype(jnp.float32) + b_ref[...].astype(jnp.float32)) + (
        c_ref[...].astype(jnp.float32) + d_ref[...].astype(jnp.float32)
    )
    rows = rows_of(halo_ref[0])
    rest = rows_of(1 - halo_ref[0])
    out_ref[rest, :] = own_ref[rest, :].astype(jnp.bfloat16)
    out_ref[rows, :] = (own_ref[rows, :] + returned).astype(jnp.bfloat16)


def struct(shape, dtype=jnp.bfloat16):
    return jax.ShapeDtypeStruct(shape, dtype)


CELL = struct((CELL_DEV, D))
CELL32 = struct((CELL_DEV, D), jnp.float32)
TILE_FLOPS = 2 * BLOCK * BLOCK * D


def call(kernel, scalars, arrays, outs, scratch=(), flops=0, mib=60):
    several = isinstance(outs, tuple)
    specs = vmem(len(outs) if several else 1)
    moved = sum(a.size * a.dtype.itemsize for a in arrays)
    return pl.pallas_call(
        kernel,
        in_specs=smem(len(scalars)) + vmem(len(arrays)),
        out_specs=specs if several else specs[0],
        out_shape=outs,
        scratch_shapes=scratch,
        cost_estimate=pl.CostEstimate(flops=flops, bytes_accessed=moved, transcendentals=0),
        compiler_params=pltpu.CompilerParams(vmem_limit_bytes=mib * 1024 * 1024),
        interpret=INTERPRET,
    )(*scalars, *arrays)


def traded(value, axis, first):
    count = lax.axis_size(axis)
    pairs = [(i, i + 1) for i in range(first, count - 1, 2)]
    return lax.ppermute(value, axis, pairs + [(b, a) for a, b in pairs])


TRADES = (("row", 1), ("row", 0), ("blk", 1), ("blk", 0))


def neighbours(values):
    received = []
    for value, (axis, first) in zip(values, TRADES):
        received.append(traded(value, axis, first))
    return received


def both_cores(value):
    count = lax.axis_size("blk")
    groups = [[i, i + 1] for i in range(0, count, 2)]
    return lax.all_gather(value, "blk", axis=0, tiled=True, axis_index_groups=groups)


def exchanged(value):
    count = lax.axis_size("blk")
    groups = [list(range(core, count, 2)) for core in range(2)]
    return lax.all_to_all(value, "blk", 0, 0, axis_index_groups=groups)


def body(
    cells,
    tile_rows,
    tile_cols,
    tile_count,
    halo_blocks,
    tile_vals,
    pool_ids,
    w_msg,
    w_query,
    cotangent,
):
    f32 = jnp.float32
    boundary = lax.dynamic_slice_in_dim(cells, halo_blocks[0] * BLOCK, BLOCK, 0)
    halos = neighbours([boundary] * 4)
    pool = pool_ids.reshape(1, CELL_DEV)
    tiles = (tile_rows, tile_cols, tile_count)
    bf16 = jnp.bfloat16
    passed, slope, table = pl.pallas_call(
        forward_kernel,
        name="forward",
        in_specs=smem(3) + vmem(5) + anywhere(3),
        out_specs=anywhere(2) + vmem(1),
        out_shape=(CELL, CELL, struct((CHIPS, SN_DEV, D))),
        scratch_shapes=[
            pltpu.VMEM((CELL_DEV, D), f32),
            pltpu.VMEM((CELL_DEV, D), bf16),
            pltpu.VMEM(tile_vals.shape, bf16),
            pltpu.VMEM((D, D), bf16),
            pltpu.VMEM((CELL_DEV, D), bf16),
            pltpu.VMEM((CELL_DEV, D), bf16),
            pltpu.SemaphoreType.DMA((5,)),
        ],
        cost_estimate=pl.CostEstimate(
            flops=20 * TILE_FLOPS, bytes_accessed=4 << 20, transcendentals=CELL_DEV * D
        ),
        compiler_params=pltpu.CompilerParams(vmem_limit_bytes=FORWARD_MIB * 1024 * 1024),
        interpret=INTERPRET,
    )(*tiles, *halos, pool, cells, tile_vals, w_msg)
    own_keys = exchanged(table).reshape(KEYS_CORE, D)
    query = call(
        query_kernel, (), (passed, w_query), CELL, flops=12 * TILE_FLOPS, mib=QUERY_MIB
    )
    own_keys, query = lax.optimization_barrier((own_keys, query))
    keys = both_cores(own_keys)
    weights = struct((2, HEADS, 2 * KEYS_CORE, CELL_DEV))
    weights, grad_own, grad_other = pl.pallas_call(
        scores_kernel,
        name="scores",
        in_specs=vmem(3),
        out_specs=hbm(1) + vmem(2),
        out_shape=(weights, CELL32, CELL),
        scratch_shapes=[
            pltpu.VMEM(weights.shape, jnp.bfloat16),
            pltpu.SemaphoreType.DMA((2, HEADS)),
        ],
        cost_estimate=pl.CostEstimate(
            flops=96 * TILE_FLOPS, bytes_accessed=8 << 20, transcendentals=weights.size
        ),
        compiler_params=pltpu.CompilerParams(vmem_limit_bytes=SCORES_MIB * 1024 * 1024),
        interpret=INTERPRET,
    )(query, cotangent, keys)
    both = both_cores(grad_other)
    chip_sum = call(
        chip_sum_kernel,
        (),
        (grad_own, both),
        struct((CHIPS, SN_DEV, D)),
        flops=TILE_FLOPS,
        mib=SUM_MIB,
    )
    parts = exchanged(chip_sum)
    attended, base = call(
        values_kernel,
        (),
        (weights, keys, cotangent, w_query),
        (CELL, CELL),
        scratch=[pltpu.VMEM((CELL_DEV, D), jnp.bfloat16)],
        flops=60 * TILE_FLOPS,
        mib=VALUES_MIB,
    )
    through, dmessage, *backs = call(
        backward_kernel,
        (tile_rows,),
        (base, parts, pool, slope, w_msg, tile_vals),
        (CELL, CELL) + (struct((BLOCK, D)),) * 4,
        flops=16 * TILE_FLOPS,
        mib=BACK_MIB,
    )
    returned = neighbours(backs)
    own = call(
        own_back_kernel,
        tiles,
        (through, dmessage, tile_vals),
        CELL32,
        flops=4 * TILE_FLOPS,
        mib=OWN_BACK_MIB,
    )
    grad_cells = call(
        final_kernel,
        (halo_blocks,),
        (own, *returned),
        CELL,
        flops=TILE_FLOPS,
        mib=FINAL_MIB,
    )
    return passed, attended, grad_cells


def solution(mesh):
    cells = P(("row", "blk"), None)
    flat = P(("row", "blk"))
    return jax.shard_map(
        body,
        mesh=mesh,
        in_specs=(
            cells,
            flat,
            flat,
            flat,
            flat,
            P(("row", "blk"), None, None),
            flat,
            P(),
            P(),
            cells,
        ),
        out_specs=(cells, cells, cells),
        check_vma=False,
    )
```

```python
import jax
import jax.numpy as jnp
from jax import lax
from jax.experimental import pallas as pl
from jax.experimental.pallas import tpu as pltpu
from jax.sharding import PartitionSpec as P

D = 768
HEADS = 12
HEAD = 64
BLOCK = 128
SN_DEV = 16
EXT = 6
CELL_DEV = 256
CHIPS = 16
KEYS_CORE = CHIPS * SN_DEV
SCALE = HEAD ** (-0.5)
INTERPRET = False
OWN_MIB = 60
FORWARD_MIB = 53
QUERY_MIB = 48
SCORES_MIB = 50
SUM_MIB = 8
VALUES_MIB = 53
BACK_MIB = 24
OWN_BACK_MIB = 24
FINAL_MIB = 24

NT = (((1,), (1,)), ((), ()))
TN = (((0,), (0,)), ((), ()))
NN = (((1,), (0,)), ((), ()))


def dot32(a, b, dims=NN):
    return lax.dot_general(a, b, dims, preferred_element_type=jnp.float32)


def vmem(count):
    return [pl.BlockSpec(memory_space=pltpu.VMEM) for _ in range(count)]


def hbm(count):
    return [pl.BlockSpec(memory_space=pltpu.HBM) for _ in range(count)]


def smem(count):
    return [pl.BlockSpec(memory_space=pltpu.SMEM) for _ in range(count)]


def rows_of(block):
    return pl.ds(pl.multiple_of(block * BLOCK, BLOCK), BLOCK)


def member_of(pool_ref):
    ids = jnp.broadcast_to(pool_ref[...], (SN_DEV, CELL_DEV))
    return ids == lax.broadcasted_iota(jnp.int32, (SN_DEV, CELL_DEV), 0)


def roots_of(member):
    return jnp.sqrt(jnp.sum(member.astype(jnp.float32), axis=1, keepdims=True))


def halo_slots():
    odd_row, odd_blk = lax.axis_index("row") % 2, lax.axis_index("blk") % 2
    return (2 + odd_row, 4 + odd_blk, 3 - odd_row, 5 - odd_blk)


def own_tiles_kernel(rows_ref, cols_ref, count_ref, cells_ref, vals_ref, acc_ref):
    acc_ref[0:BLOCK, :] = dot32(vals_ref[0], cells_ref[0:BLOCK, :])
    acc_ref[BLOCK:, :] = dot32(vals_ref[1], cells_ref[BLOCK:, :])

    def add_tile(number, carry):
        picked = cells_ref[rows_of(cols_ref[number]), :]
        acc_ref[rows_of(rows_ref[number]), :] += dot32(vals_ref[number], picked)
        return carry

    lax.fori_loop(EXT, count_ref[0], add_tile, 0)


def forward_kernel(
    rows_ref,
    own_ref,
    cells_ref,
    halo0_ref,
    halo1_ref,
    halo2_ref,
    halo3_ref,
    vals_ref,
    pool_ref,
    w_msg_ref,
    passed_ref,
    slope_ref,
    table_ref,
    acc_ref,
):
    acc_ref[...] = own_ref[...]
    for slot, ref in zip(halo_slots(), (halo0_ref, halo1_ref, halo2_ref, halo3_ref)):
        acc_ref[rows_of(rows_ref[slot]), :] += dot32(vals_ref[slot], ref[...])
    hidden = dot32(acc_ref[...].astype(jnp.bfloat16), w_msg_ref[...])
    sigma = 1.0 / (1.0 + jnp.exp(-hidden))
    slope_ref[...] = (sigma * (1.0 + hidden * (1.0 - sigma))).astype(jnp.bfloat16)
    passed = (cells_ref[...].astype(jnp.float32) + hidden * sigma).astype(jnp.bfloat16)
    passed_ref[...] = passed
    member = member_of(pool_ref)
    pooled = dot32(member.astype(jnp.bfloat16), passed)
    supern = (pooled / roots_of(member)).astype(jnp.bfloat16)
    for chip in range(CHIPS):
        table_ref[chip] = supern


def query_kernel(passed_ref, w_query_ref, query_ref):
    query_ref[...] = (dot32(passed_ref[...], w_query_ref[...]) * SCALE).astype(jnp.bfloat16)


def half_lanes(value, half):
    lanes = lax.broadcasted_iota(jnp.int32, value.shape, 1)
    inside = (lanes >= half * HEAD) & (lanes < (half + 1) * HEAD)
    return jnp.where(inside, value, jnp.zeros_like(value))


def pair_cols(pair):
    return slice(pair * 2 * HEAD, (pair + 1) * 2 * HEAD)


def scores_kernel(
    query_ref,
    cot_ref,
    keys_ref,
    weights_ref,
    grad_own_ref,
    grad_other_ref,
    weights_buf,
    sems,
):
    first = lax.axis_index("blk") % 2 == 0
    copies = []
    for pair in range(HEADS // 2):
        cols = pair_cols(pair)
        keys = keys_ref[:, cols]
        key_grad = None
        for half in range(2):
            head = 2 * pair + half
            q = half_lanes(query_ref[:, cols], half)
            g = half_lanes(cot_ref[:, cols], half)
            scores = dot32(keys, q, NT)
            slope = dot32(keys, g, NT)
            probs = jnp.exp(scores - jnp.max(scores, axis=0, keepdims=True))
            probs = probs * (1.0 / jnp.sum(probs, axis=0, keepdims=True))
            rounded = probs.astype(jnp.bfloat16)
            centre = jnp.sum(rounded.astype(jnp.float32) * slope, axis=0, keepdims=True)
            dscore = (probs * (slope - centre)).astype(jnp.bfloat16)
            for kind, weights in enumerate((rounded, dscore)):
                weights_buf[kind, head] = weights
                copy = pltpu.make_async_copy(
                    weights_buf.at[kind, head], weights_ref.at[kind, head], sems.at[kind, head]
                )
                copy.start()
                copies.append(copy)
            part = dot32(dscore, q) + dot32(rounded, g)
            key_grad = part if key_grad is None else key_grad + part
        low, high = key_grad[:KEYS_CORE], key_grad[KEYS_CORE:]
        grad_own_ref[:, cols] = jnp.where(first, low, high)
        grad_other_ref[:, cols] = jnp.where(first, high, low).astype(jnp.bfloat16)
    for copy in copies:
        copy.wait()


def chip_sum_kernel(own_ref, both_ref, out_ref):
    partner = (1 - lax.axis_index("blk") % 2) * KEYS_CORE
    for chip in range(CHIPS):
        start = chip * SN_DEV
        received = both_ref[pl.ds(pl.multiple_of(partner + start, SN_DEV), SN_DEV), :]
        total = own_ref[start : start + SN_DEV, :] + received.astype(jnp.float32)
        out_ref[chip] = total.astype(jnp.bfloat16)


def values_kernel(
    weights_ref,
    keys_ref,
    cot_ref,
    w_query_ref,
    attended_ref,
    base_ref,
    dquery_ref,
):
    for pair in range(HEADS // 2):
        cols = pair_cols(pair)
        keys_t = keys_ref[:, cols].T
        values, dquery = [], []
        for half in range(2):
            head = 2 * pair + half
            head_t = keys_t[half * HEAD : (half + 1) * HEAD, :]
            values.append(dot32(head_t, weights_ref[0, head]))
            dquery.append(dot32(head_t, weights_ref[1, head]))
        attended_ref[:, cols] = jnp.concatenate(values, axis=0).T.astype(jnp.bfloat16)
        dquery_ref[:, cols] = (jnp.concatenate(dquery, axis=0) * SCALE).T.astype(jnp.bfloat16)
    back = dot32(dquery_ref[...], w_query_ref[...], NT)
    base_ref[...] = (cot_ref[...].astype(jnp.float32) + back).astype(jnp.bfloat16)


def backward_kernel(
    rows_ref,
    base_ref,
    parts_ref,
    pool_ref,
    slope_ref,
    w_msg_ref,
    vals_ref,
    through_ref,
    dmsg_ref,
    back0_ref,
    back1_ref,
    back2_ref,
    back3_ref,
):
    key_grad = jnp.sum(parts_ref[...].astype(jnp.float32), axis=0)
    member = member_of(pool_ref)
    pool_grad = (key_grad / roots_of(member)).astype(jnp.bfloat16)
    spread = dot32(member.astype(jnp.bfloat16), pool_grad, TN)
    through = (base_ref[...].astype(jnp.float32) + spread).astype(jnp.bfloat16)
    through_ref[...] = through
    slope = slope_ref[...].astype(jnp.float32)
    dhidden = (through.astype(jnp.float32) * slope).astype(jnp.bfloat16)
    dmsg_ref[...] = dot32(dhidden, w_msg_ref[...], NT).astype(jnp.bfloat16)
    for slot, ref in zip(halo_slots(), (back0_ref, back1_ref, back2_ref, back3_ref)):
        picked = dmsg_ref[rows_of(rows_ref[slot]), :]
        ref[...] = dot32(vals_ref[slot], picked, TN).astype(jnp.bfloat16)


def own_back_kernel(rows_ref, cols_ref, count_ref, through_ref, dmsg_ref, vals_ref, own_ref):
    through = through_ref[...].astype(jnp.float32)
    own_ref[0:BLOCK, :] = through[0:BLOCK] + dot32(vals_ref[0], dmsg_ref[0:BLOCK, :], TN)
    own_ref[BLOCK:, :] = through[BLOCK:] + dot32(vals_ref[1], dmsg_ref[BLOCK:, :], TN)

    def back_tile(number, carry):
        picked = dmsg_ref[rows_of(rows_ref[number]), :]
        own_ref[rows_of(cols_ref[number]), :] += dot32(vals_ref[number], picked, TN)
        return carry

    lax.fori_loop(EXT, count_ref[0], back_tile, 0)


def final_kernel(halo_ref, own_ref, a_ref, b_ref, c_ref, d_ref, out_ref):
    returned = (a_ref[...].astype(jnp.float32) + b_ref[...].astype(jnp.float32)) + (
        c_ref[...].astype(jnp.float32) + d_ref[...].astype(jnp.float32)
    )
    rows = rows_of(halo_ref[0])
    rest = rows_of(1 - halo_ref[0])
    out_ref[rest, :] = own_ref[rest, :].astype(jnp.bfloat16)
    out_ref[rows, :] = (own_ref[rows, :] + returned).astype(jnp.bfloat16)


def struct(shape, dtype=jnp.bfloat16):
    return jax.ShapeDtypeStruct(shape, dtype)


CELL = struct((CELL_DEV, D))
CELL32 = struct((CELL_DEV, D), jnp.float32)
TILE_FLOPS = 2 * BLOCK * BLOCK * D


def call(kernel, scalars, arrays, outs, scratch=(), flops=0, mib=60):
    several = isinstance(outs, tuple)
    specs = vmem(len(outs) if several else 1)
    moved = sum(a.size * a.dtype.itemsize for a in arrays)
    return pl.pallas_call(
        kernel,
        in_specs=smem(len(scalars)) + vmem(len(arrays)),
        out_specs=specs if several else specs[0],
        out_shape=outs,
        scratch_shapes=scratch,
        cost_estimate=pl.CostEstimate(flops=flops, bytes_accessed=moved, transcendentals=0),
        compiler_params=pltpu.CompilerParams(vmem_limit_bytes=mib * 1024 * 1024),
        interpret=INTERPRET,
    )(*scalars, *arrays)


def traded(value, axis, first):
    count = lax.axis_size(axis)
    pairs = [(i, i + 1) for i in range(first, count - 1, 2)]
    return lax.ppermute(value, axis, pairs + [(b, a) for a, b in pairs])


TRADES = (("row", 1), ("blk", 1), ("row", 0), ("blk", 0))


def neighbours(values):
    received = []
    for value, (axis, first) in zip(values, TRADES):
        received.append(traded(value, axis, first))
    return received


def both_cores(value):
    count = lax.axis_size("blk")
    groups = [[i, i + 1] for i in range(0, count, 2)]
    return lax.all_gather(value, "blk", axis=0, tiled=True, axis_index_groups=groups)


def exchanged(value):
    count = lax.axis_size("blk")
    groups = [list(range(core, count, 2)) for core in range(2)]
    return lax.all_to_all(value, "blk", 0, 0, axis_index_groups=groups)


def body(
    cells,
    tile_rows,
    tile_cols,
    tile_count,
    halo_blocks,
    tile_vals,
    pool_ids,
    w_msg,
    w_query,
    cotangent,
):
    f32 = jnp.float32
    boundary = lax.dynamic_slice_in_dim(cells, halo_blocks[0] * BLOCK, BLOCK, 0)
    halos = neighbours([boundary] * 4)
    pool = pool_ids.reshape(1, CELL_DEV)
    tiles = (tile_rows, tile_cols, tile_count)
    own_message = call(
        own_tiles_kernel,
        tiles,
        (cells, tile_vals),
        CELL32,
        flops=4 * TILE_FLOPS,
        mib=OWN_MIB,
    )
    passed, slope, table = call(
        forward_kernel,
        (tile_rows,),
        (own_message, cells, *halos, tile_vals, pool, w_msg),
        (CELL, CELL, struct((CHIPS, SN_DEV, D))),
        scratch=[pltpu.VMEM((CELL_DEV, D), f32)],
        flops=16 * TILE_FLOPS,
        mib=FORWARD_MIB,
    )
    own_keys = exchanged(table).reshape(KEYS_CORE, D)
    query = call(
        query_kernel, (), (passed, w_query), CELL, flops=12 * TILE_FLOPS, mib=QUERY_MIB
    )
    own_keys, query = lax.optimization_barrier((own_keys, query))
    keys = both_cores(own_keys)
    weights = struct((2, HEADS, 2 * KEYS_CORE, CELL_DEV))
    weights, grad_own, grad_other = pl.pallas_call(
        scores_kernel,
        name="scores",
        in_specs=vmem(3),
        out_specs=hbm(1) + vmem(2),
        out_shape=(weights, CELL32, CELL),
        scratch_shapes=[
            pltpu.VMEM(weights.shape, jnp.bfloat16),
            pltpu.SemaphoreType.DMA((2, HEADS)),
        ],
        cost_estimate=pl.CostEstimate(
            flops=96 * TILE_FLOPS, bytes_accessed=8 << 20, transcendentals=weights.size
        ),
        compiler_params=pltpu.CompilerParams(vmem_limit_bytes=SCORES_MIB * 1024 * 1024),
        interpret=INTERPRET,
    )(query, cotangent, keys)
    both = both_cores(grad_other)
    chip_sum = call(
        chip_sum_kernel,
        (),
        (grad_own, both),
        struct((CHIPS, SN_DEV, D)),
        flops=TILE_FLOPS,
        mib=SUM_MIB,
    )
    parts = exchanged(chip_sum)
    attended, base = call(
        values_kernel,
        (),
        (weights, keys, cotangent, w_query),
        (CELL, CELL),
        scratch=[pltpu.VMEM((CELL_DEV, D), jnp.bfloat16)],
        flops=60 * TILE_FLOPS,
        mib=VALUES_MIB,
    )
    through, dmessage, *backs = call(
        backward_kernel,
        (tile_rows,),
        (base, parts, pool, slope, w_msg, tile_vals),
        (CELL, CELL) + (struct((BLOCK, D)),) * 4,
        flops=16 * TILE_FLOPS,
        mib=BACK_MIB,
    )
    returned = neighbours(backs)
    own = call(
        own_back_kernel,
        tiles,
        (through, dmessage, tile_vals),
        CELL32,
        flops=4 * TILE_FLOPS,
        mib=OWN_BACK_MIB,
    )
    grad_cells = call(
        final_kernel,
        (halo_blocks,),
        (own, *returned),
        CELL,
        flops=TILE_FLOPS,
        mib=FINAL_MIB,
    )
    return passed, attended, grad_cells


def solution(mesh):
    cells = P(("row", "blk"), None)
    flat = P(("row", "blk"))
    return jax.shard_map(
        body,
        mesh=mesh,
        in_specs=(
            cells,
            flat,
            flat,
            flat,
            flat,
            P(("row", "blk"), None, None),
            flat,
            P(),
            P(),
            cells,
        ),
        out_specs=(cells, cells, cells),
        check_vma=False,
    )
```
